256 devices in a mesh: sky: 64 (over z, y, core), rep: 4 (over x).
Axes of the slice: x: 4, y: 4, z: 8, core: 2. Of those that a mesh axis runs over, the one named last changes fastest.
Arguments:
- saved_acts: bfloat16 [64, 1024, 2048], P('rep', 'sky'), parts along dimension 0, may hold values from -4 to 4
- scales: float32 [64, 1024, 16], P('rep', 'sky'), parts along dimension 0, may hold values from 0.2 to 4
- grad_out: bfloat16 [64, 1024, 2048], P('rep', 'sky'), parts along dimension 0, may hold values from -6 to 6
- weights: bfloat16 [5, 16, 16], replicated, may hold values from -0.625 to 0.625
- edge_up: int32 [64, 3, 2048], P('sky'), may hold values from 0 to 2048, as said below
- edge_down: int32 [64, 3, 2048], P('sky'), may hold values from 0 to 2048, as said below
Outputs:
- grad_in: bfloat16 [64, 1024, 2048], P('rep', 'sky'), parts along dimension 0
- weight_grad: float32 [20, 16, 16], P('rep'), parts along dimension 0
The draws below stay inside these ranges and needn't reach their ends.
There are 4 independent parts, one for each index of `rep`. The reference program is written for one: setup_inputs(seed, part) draws one part's arguments, and reference() takes and returns one part's arrays. A program takes and returns all parts, laid end to end along the dimension named above; an argument that names none is the same for every part. Nothing has to cross between parts.
Inputs may be any that keep to these rules, and one draw needn't show every extreme that they name: edge_down[t, j, c] is the column of tile t+1's first row (tile 0 after the last) linked to column c of tile t's last row, or 2048 where there is none; the links are mutual: edge_up of tile t+1 lists exactly the reverse links. edge_up[t, j, c] is the column of tile t-1's last row (the last tile before tile 0) linked to column c of tile t's first row, or 2048 where there is none.
All inputs are finite; a program needn't handle non-finite values.
Results may differ from the reference program's by a relative error of at most 0.0028.
Values sent between devices are 32-bit elements; how exact they have to be, the bound alone decides.
A program may use at most 192 MiB of HBM per device.

```python
import math
import jax
import jax.numpy as jnp

C = 16
ORDER = 5
COLS = 2048
ROWS = 16
TILES = 64
NROWS = 1024
BLOCKS = 16
NPIX = 2097152


def boundary_offsets(key):
    base_key = jax.random.fold_in(key, 7)
    magnitude = jax.random.randint(base_key, (TILES,), 1, COLS // 4 + 1)
    direction = jax.random.randint(jax.random.fold_in(base_key, 1), (TILES,), 0, 2) * 2 - 1
    return magnitude * direction


def link_table(offsets, sign):
    columns = jnp.arange(COLS, dtype=jnp.int32)
    steps_off = jnp.arange(3, dtype=jnp.int32) - 1
    target = columns[None, None, :] + sign * (offsets[:, None, None] + steps_off[None, :, None])
    inside = (target >= 0) & (target < COLS)
    return jnp.where(inside, target, COLS).astype(jnp.int32)


def draw_edge_down(key, part):
    return link_table(boundary_offsets(key), 1)


def draw_edge_up(key, part):
    return link_table(jnp.roll(boundary_offsets(key), 1), -1)


def steps_of(own_key, extent, split, low, largest):
    level = 1.0
    for position, shards_of in split:
        draws = jax.random.uniform(jax.random.fold_in(jax.random.fold_in(own_key, 6), position), (shards_of,), jnp.float32, low / len(split), largest / len(split))
        level = level * jnp.repeat(jnp.exp(draws), extent[position] // shards_of).reshape((-1,) + (1,) * (len(extent) - 1 - position))
    return level


def scatter_about(own_key, extent, deviation, most, shards=(), kind=jnp.bfloat16):
    drawn = jax.random.normal(own_key, extent, jnp.float32) * deviation
    if len(shards) > 0:
        drawn = steps_of(own_key, extent, shards, -0.22, 0.18) * drawn
    return jnp.clip(drawn, min=-most, max=most).astype(kind)


def setup_inputs(seed: int = 0, part: int = 0) -> dict:
    keys = jax.random.split(jax.random.key(seed), 7)
    own_keys = jax.random.split(jax.random.fold_in(keys[6], part), 7)
    saved_acts = scatter_about(own_keys[0], (C, NROWS, COLS), 1.0, 4.0, ((1, 64),))
    scales = jnp.clip(jnp.exp(math.log(4.0) - 2.9957323 * jax.random.uniform(own_keys[1], (C, NROWS, BLOCKS), jnp.float32) ** steps_of(own_keys[1], (C, NROWS, BLOCKS), ((1, 64),), -0.2, 0.2)), 0.2, 4.0)
    grad_out = scatter_about(own_keys[2], (C, NROWS, COLS), 1.0, 6.0, ((1, 64),))
    weights = scatter_about(keys[3], (ORDER, C, C), (C * ORDER) ** -0.5, 0.625)
    edge_up = draw_edge_up(jax.random.fold_in(keys[6], 71), part)
    edge_down = draw_edge_down(jax.random.fold_in(keys[6], 71), part)
    return dict(saved_acts=saved_acts, scales=scales, grad_out=grad_out, weights=weights, edge_up=edge_up, edge_down=edge_down)


def triple(field_rows):
    padded = jnp.pad(field_rows, ((0, 0), (0, 0), (1, 1)))
    return padded[:, :, :-2] + padded[:, :, 1:-1] + padded[:, :, 2:]

def linked(edge_rows, link_lists):
    summed = jnp.zeros(edge_rows.shape, jnp.float32)
    for column in range(3):
        link_index = link_lists[:, column, :]
        clipped = jnp.broadcast_to(jnp.minimum(link_index, COLS - 1)[None], edge_rows.shape)
        picked = jnp.take_along_axis(edge_rows, clipped, axis=2)
        summed = summed + jnp.where((link_index < COLS)[None], picked, 0.0)
    return summed

def operate(state, edge_up, edge_down):
    row_above = jnp.roll(state, 1, axis=1)
    row_below = jnp.roll(state, -1, axis=1)
    vert_above = triple(row_above)
    vert_below = triple(row_below)
    vert_above = vert_above.at[:, ::ROWS].set(linked(row_above[:, ::ROWS], edge_up))
    vert_below = vert_below.at[:, ROWS - 1::ROWS].set(linked(row_below[:, ROWS - 1::ROWS], edge_down))
    sideways = triple(state) - state
    return -0.125 * (vert_above + vert_below + sideways)

def reference(saved_acts, scales, grad_out, weights, edge_up, edge_down):
    activation = (saved_acts.astype(jnp.float32).reshape(C, NROWS, BLOCKS, 128) * scales[..., None]).reshape(C, NROWS, COLS)
    norm_factor = 1.0 / math.sqrt(NPIX)
    grad_wide = grad_out.astype(jnp.float32)
    grads = []
    older = activation
    newer = activation
    for degree in range(ORDER):
        if degree == 1:
            older, newer = (activation, operate(activation, edge_up, edge_down))
        elif degree >= 2:
            older, newer = (newer, 2.0 * operate(newer, edge_up, edge_down) - older)
        rounded = newer.astype(jnp.bfloat16).astype(jnp.float32)
        grads.append(jnp.einsum('irc,orc->io', rounded, grad_wide) * norm_factor)
    weight_grad = jnp.stack(grads)
    weights_wide = weights.astype(jnp.float32)

    def coeff(degree):
        return jnp.einsum('io,orc->irc', weights_wide[degree], grad_wide)
    current = coeff(ORDER - 1)
    previous = jnp.zeros_like(current)
    for degree in range(ORDER - 2, 0, -1):
        updated = coeff(degree) + 2.0 * operate(current, edge_up, edge_down) - previous
        previous, current = (current, updated)
    grad_in = coeff(0) + operate(current, edge_up, edge_down) - previous
    return (grad_in.astype(jnp.bfloat16), weight_grad)
```

```python
import functools
import math

import jax
import jax.numpy as jnp
from jax import lax
from jax.experimental import pallas as pl
from jax.experimental.pallas import tpu as pltpu
from jax.sharding import PartitionSpec as P

F32 = jnp.float32
BF16 = jnp.bfloat16
LANES = 128
HALO = 4
MESH = pl.DeviceIdType.MESH
CONTRACT_LAST = (((1,), (1,)), ((), ()))


def split_bf16(value):
    high = value.astype(BF16)
    low = (value - high.astype(F32)).astype(BF16)
    return high, low


def remote(source, target, send, recv, peer):
    return pltpu.make_async_remote_copy(
        src_ref=source, dst_ref=target, send_sem=send, recv_sem=recv,
        device_id={"sky": peer}, device_id_type=MESH,
    )


def sweep_row(order, upper, middle, lower, older, link=None, field=None, split=None):
    channels, columns = middle.shape
    blocks = columns // LANES
    lane = lax.broadcasted_iota(jnp.int32, (channels, LANES), 1)
    sums = []
    for block in range(blocks):
        lanes = slice(block * LANES, (block + 1) * LANES)
        value = middle[:, lanes]
        if upper is not None:
            value = value + upper[:, lanes]
        if lower is not None:
            value = value + lower[:, lanes]
        sums.append(value)
    right_moved = [pltpu.roll(value, 1, 1) for value in sums]
    left_moved = [pltpu.roll(value, LANES - 1, 1) for value in sums]
    for block in range(blocks):
        lanes = slice(block * LANES, (block + 1) * LANES)
        from_left = jnp.where(lane == 0, right_moved[block - 1] if block > 0 else 0.0, right_moved[block])
        from_right = jnp.where(
            lane == LANES - 1, left_moved[block + 1] if block < blocks - 1 else 0.0, left_moved[block]
        )
        total = sums[block] + from_left + from_right - middle[:, lanes]
        if link is not None:
            total = total + link[:, lanes]
        if order == 1:
            result = -0.125 * total
        else:
            result = -0.25 * total - older[:, lanes]
        if field is not None:
            field[:, lanes] = result
        if split is not None:
            high, low = split_bf16(result)
            split[channels * order : channels * (order + 1), lanes] = high
            start = channels * (HALO + order)
            split[start : start + channels, lanes] = low


def stacked_weights(weights):
    orders = weights.shape[0]
    return jnp.concatenate(
        [weights[k] for k in range(orders)] + [weights[k] for k in range(1, orders)], axis=1
    )


def block_list(table, homes, slots, which):
    blocks = table.shape[1] // LANES
    for entry in range(3):
        for block in range(blocks):
            homes[entry, block : block + 1, :] = jnp.right_shift(
                table[entry : entry + 1, block * LANES : (block + 1) * LANES], 7
            )
    home = [homes[entry] for entry in range(3)]

    def lowest(candidates):
        least = functools.reduce(jnp.minimum, candidates)
        return jnp.min(least, axis=1, keepdims=True)

    first = lowest(home)
    second = lowest([jnp.where(value > first, value, blocks) for value in home])
    third = lowest([jnp.where(value > second, value, blocks) for value in home])
    lane = lax.broadcasted_iota(jnp.int32, (blocks, LANES), 1)
    more = jnp.max((third < blocks).astype(jnp.int32), axis=0, keepdims=True)
    slots[which] = jnp.where(
        lane == 0,
        jnp.minimum(first, blocks - 1),
        jnp.where(lane == 1, jnp.minimum(second, blocks - 1), more),
    )


def exchange_kernel(
    sky,
    saved, scales, grad, weights, up, down,
    fields, edge_acts, inner_grad, sums, slots, tables,
    flat, acts, split, homes, halo_send, halo_recv, table_send, table_recv,
):
    channels, rows, columns = saved.shape
    orders = weights.shape[0]
    me = lax.axis_index("sky")
    before = lax.rem(me + sky - 1, sky)
    after = lax.rem(me + 1, sky)

    barrier = pltpu.get_barrier_semaphore()
    for peer in (before, after):
        pl.semaphore_signal(barrier, inc=1, device_id={"sky": peer}, device_id_type=MESH)

    for channel in range(channels):
        flat[channel] = grad[channel].astype(F32)
    edge_first = [r for i in range(HALO) for r in (rows - 1 - i, i)]
    for r in edge_first:
        fields[0, HALO + r] = flat[:, r, :]
    pl.semaphore_wait(barrier, 2)

    copies = [
        remote(up.at[0], tables.at[1], table_send.at[0], table_recv.at[0], before),
        remote(down.at[0], tables.at[0], table_send.at[1], table_recv.at[1], after),
    ]
    for i in range(HALO):
        copies += [
            remote(fields.at[0, HALO + i], fields.at[0, HALO + rows + i], halo_send.at[0, i], halo_recv.at[0, i], before),
            remote(fields.at[0, HALO + rows - 1 - i], fields.at[0, HALO - 1 - i], halo_send.at[1, i], halo_recv.at[1, i], after),
        ]
    for copy in copies:
        copy.start()

    for r in range(HALO, rows - HALO):
        value = flat[:, r, :]
        fields[0, HALO + r] = value
        split[r, 0:channels] = value.astype(BF16)

    for order in range(1, orders):
        @pl.loop(order, rows - order, step=2)
        def _(start):
            for r in (start, start + 1):
                row = HALO + r
                sweep_row(
                    order, fields.at[order - 1, row - 1], fields.at[order - 1, row], fields.at[order - 1, row + 1],
                    fields.at[order - 2, row] if order > 1 else None,
                    field=fields.at[order, row] if order < orders - 1 else None, split=split.at[r],
                )

    blocks = scales.shape[2]
    width = columns // blocks

    @pl.loop(0, channels)
    def _(channel):
        scale = scales[channel]
        for block in range(blocks):
            lanes = slice(block * width, (block + 1) * width)
            flat[channel, :, lanes] = saved[channel, :, lanes].astype(F32) * scale[:, block : block + 1]

    for r in range(rows):
        high, low = split_bf16(flat[:, r, :])
        if r < HALO:
            target = edge_acts.at[r]
        elif r >= rows - HALO:
            target = edge_acts.at[r - rows + 2 * HALO]
        else:
            target = acts.at[r - HALO]
        target[0:channels] = high
        target[channels : 2 * channels] = low

    sums[...] = jnp.zeros_like(sums)
    left = stacked_weights(weights)
    for r in range(HALO, rows - HALO):
        sums[...] += lax.dot_general(acts[r - HALO], split[r], CONTRACT_LAST, preferred_element_type=F32)
        inner_grad[r - HALO] = jnp.dot(left, split[r], preferred_element_type=F32)

    block_list(up.at[0], homes, slots, 0)
    block_list(down.at[0], homes, slots, 1)
    for copy in copies[:2]:
        copy.wait()
    block_list(tables.at[0], homes, slots, 2)
    block_list(tables.at[1], homes, slots, 3)
    for copy in copies[2:]:
        copy.wait()


def linked_row(source, table, slots, which, target):
    channels, columns = source.shape
    blocks = columns // LANES

    def source_block(origin):
        return source[:, pl.ds(pl.multiple_of(origin * LANES, LANES), LANES)]

    def indices(out_lanes):
        for entry in range(3):
            index = jnp.broadcast_to(table[entry : entry + 1, out_lanes], (channels, LANES))
            yield jnp.right_shift(index, 7), jnp.bitwise_and(index, LANES - 1)

    def moved(values, lane):
        return jnp.take_along_axis(values, lane, axis=1, mode="promise_in_bounds")

    for block in range(blocks):
        out_lanes = slice(block * LANES, (block + 1) * LANES)
        first, second = slots[which, block, 0], slots[which, block, 1]
        low, high = source_block(first), source_block(second)
        total = None
        for home, lane in indices(out_lanes):
            picked = jnp.where(home == first, moved(low, lane), jnp.where(home == second, moved(high, lane), 0.0))
            total = picked if total is None else total + picked
        target[:, out_lanes] = total

    @pl.when(slots[which, 0, 2] > 0)
    def _():
        @pl.loop(0, blocks)
        def _(block):
            out_lanes = pl.ds(pl.multiple_of(block * LANES, LANES), LANES)

            def add(origin, total):
                values = source_block(origin)
                for home, lane in indices(out_lanes):
                    total = total + jnp.where(home == origin, moved(values, lane), 0.0)
                return total

            target[:, out_lanes] = lax.fori_loop(0, blocks, add, jnp.zeros((channels, LANES), F32))


def edge_kernel(
    fields, edge_acts, inner_grad, inner_sums, slots, tables, up, down, weights,
    out, local,
    fresh, split, links, flat,
):
    channels, rows, columns = out.shape
    orders = weights.shape[0]
    top = HALO
    bottom = HALO + rows - 1
    mirror = 2 * HALO + rows - 1

    def edge(r):
        return r if r < HALO else r - rows + 2 * HALO

    def field(order, row):
        if order == 0 or HALO + order <= row <= bottom - order:
            return fields.at[order, row]
        at = row - order if row <= HALO + order else HALO + row - (mirror - HALO - order + 1)
        return fresh.at[order - 1, at]

    for r in range(HALO, rows - HALO):
        flat[:, r, :] = inner_grad[r - HALO]
    for r in list(range(HALO)) + list(range(rows - HALO, rows)):
        depth = min(r, rows - 1 - r)
        split[edge(r), 0:channels] = fields[0, HALO + r].astype(BF16)
        for order in range(1, depth + 1):
            high, low = split_bf16(fields[order, HALO + r])
            split[edge(r), channels * order : channels * (order + 1)] = high
            split[edge(r), channels * (HALO + order) : channels * (HALO + order + 1)] = low

    for order in range(1, orders):
        last = order == orders - 1
        linked_row(field(order - 1, top - 1), up.at[0], slots, 0, links.at[0])
        linked_row(field(order - 1, bottom + 1), down.at[0], slots, 1, links.at[1])
        if not last:
            linked_row(field(order - 1, top), tables.at[0], slots, 2, links.at[2])
            linked_row(field(order - 1, bottom), tables.at[1], slots, 3, links.at[3])
        for near in range(order, HALO + order):
            for row in (near, mirror - near):
                upper, lower, link = field(order - 1, row - 1), field(order - 1, row + 1), None
                if row == top:
                    upper, link = None, links.at[0]
                elif row == bottom:
                    lower, link = None, links.at[1]
                elif row == top - 1:
                    lower, link = None, links.at[2]
                elif row == bottom + 1:
                    upper, link = None, links.at[3]
                sweep_row(
                    order, upper, field(order - 1, row), lower, field(order - 2, row) if order > 1 else None,
                    link=link, field=None if last else field(order, row),
                    split=split.at[edge(row - HALO)] if top <= row <= bottom else None,
                )

    sums = inner_sums[...]
    for r in range(2 * HALO):
        sums += lax.dot_general(edge_acts[r], split[r], CONTRACT_LAST, preferred_element_type=F32)
    lane = lax.broadcasted_iota(jnp.int32, (channels, LANES), 1)
    both = sums[0:channels] + sums[channels : 2 * channels]
    first = both[:, 0:LANES]
    second = jnp.concatenate([both[:, LANES:], jnp.zeros((channels, 2 * LANES - both.shape[1]), F32)], axis=1)
    moved = jnp.where(lane < LANES // 2, pltpu.roll(first, LANES // 2, 1), pltpu.roll(second, LANES // 2, 1))
    wide = channels * orders
    local[...] = jnp.where(lane < wide, first, 0.0) + jnp.where((lane >= channels) & (lane < wide), moved, 0.0)

    left = stacked_weights(weights)
    for r in list(range(HALO)) + list(range(rows - HALO, rows)):
        flat[:, r, :] = jnp.dot(left, split[edge(r)], preferred_element_type=F32)
    for channel in range(channels):
        out[channel] = flat[channel].astype(BF16)


def sum_kernel(sky, inner, norm, local, weight_grad, part_in, part_out, in_send, in_recv, out_send, out_recv):
    orders, channels = weight_grad.shape[:2]
    outer = sky // inner
    me = lax.axis_index("sky")
    slot = lax.rem(me, inner)
    group = lax.div(me, inner)

    def in_peer(step):
        return group * inner + lax.rem(slot + step, inner)

    def out_peer(step):
        return lax.rem(group + step, outer) * inner + slot

    barrier = pltpu.get_barrier_semaphore()
    peers = [in_peer(step) for step in range(1, inner)] + [out_peer(step) for step in range(1, outer)]
    for peer in peers:
        pl.semaphore_signal(barrier, inc=1, device_id={"sky": peer}, device_id_type=MESH)
    part_in[slot] = local[...]
    pl.semaphore_wait(barrier, len(peers))

    def exchange(buffer, own, count, peer_of, send, recv):
        copies = [
            remote(buffer.at[own], buffer.at[own], send.at[step], recv.at[step], peer_of(step))
            for step in range(1, count)
        ]
        for copy in copies:
            copy.start()
        for copy in copies:
            copy.wait()
        return functools.reduce(lambda total, i: total + buffer[i], range(1, count), buffer[0])

    part_out[group] = exchange(part_in, slot, inner, in_peer, in_send, in_recv)
    total = exchange(part_out, group, outer, out_peer, out_send, out_recv) * norm
    for k in range(orders):
        weight_grad[k] = total[:, channels * k : channels * (k + 1)]


def on_device(sky, saved_acts, scales, grad_out, weights, edge_up, edge_down):
    channels, rows, columns = saved_acts.shape
    orders = weights.shape[0]
    inner = min(8, sky)
    outer = sky // inner
    norm = 1.0 / math.sqrt(rows * columns * sky)
    stacked = channels * (2 * orders - 1)
    vmem = pl.BlockSpec(memory_space=pltpu.VMEM)
    smem = pl.BlockSpec(memory_space=pltpu.SMEM)
    dma = pltpu.SemaphoreType.DMA
    shape = jax.ShapeDtypeStruct
    fields, edge_acts, inner_grad, sums, slots, tables = pl.pallas_call(
        functools.partial(exchange_kernel, sky),
        out_shape=(
            shape((orders - 1, rows + 2 * HALO, channels, columns), F32),
            shape((2 * HALO, 2 * channels, columns), BF16),
            shape((rows - 2 * HALO, channels, columns), F32),
            shape((2 * channels, stacked), F32),
            shape((4, columns // LANES, LANES), jnp.int32),
            shape((2, 3, columns), jnp.int32),
        ),
        in_specs=[vmem] * 6,
        out_specs=(vmem,) * 6,
        scratch_shapes=[
            pltpu.VMEM((channels, rows, columns), F32),
            pltpu.VMEM((rows - 2 * HALO, 2 * channels, columns), BF16),
            pltpu.VMEM((rows, stacked, columns), BF16),
            pltpu.VMEM((3, columns // LANES, LANES), jnp.int32),
            dma((2, HALO)), dma((2, HALO)), dma((2,)), dma((2,)),
        ],
        compiler_params=pltpu.CompilerParams(
            collective_id=0, has_side_effects=True, vmem_limit_bytes=32 * 2**20
        ),
        name="exchange",
    )(saved_acts, scales, grad_out, weights, edge_up, edge_down)
    grad_in, local = pl.pallas_call(
        edge_kernel,
        out_shape=(shape((channels, rows, columns), BF16), shape((channels, LANES), F32)),
        in_specs=[vmem] * 4 + [smem] + [vmem] * 4,
        out_specs=(vmem, vmem),
        scratch_shapes=[
            pltpu.VMEM((orders - 2, 2 * HALO, channels, columns), F32),
            pltpu.VMEM((2 * HALO, stacked, columns), BF16),
            pltpu.VMEM((4, channels, columns), F32),
            pltpu.VMEM((channels, rows, columns), F32),
        ],
        compiler_params=pltpu.CompilerParams(vmem_limit_bytes=32 * 2**20),
        name="edges",
    )(fields, edge_acts, inner_grad, sums, slots, tables, edge_up, edge_down, weights)
    weight_grad = pl.pallas_call(
        functools.partial(sum_kernel, sky, inner, norm),
        out_shape=shape((orders, channels, channels), F32),
        in_specs=[vmem],
        out_specs=vmem,
        scratch_shapes=[
            pltpu.VMEM((inner, channels, LANES), F32),
            pltpu.VMEM((outer, channels, LANES), F32),
            dma((inner,)), dma((inner,)), dma((outer,)), dma((outer,)),
        ],
        compiler_params=pltpu.CompilerParams(collective_id=1, has_side_effects=True),
        name="sky_sum",
    )(local)
    return grad_in, weight_grad


def solution(mesh):
    return jax.shard_map(
        functools.partial(on_device, mesh.shape["sky"]),
        mesh=mesh,
        in_specs=(
            P("rep", "sky", None),
            P("rep", "sky", None),
            P("rep", "sky", None),
            P(),
            P("sky", None, None),
            P("sky", None, None),
        ),
        out_specs=(P("rep", "sky", None), P("rep", None, None)),
        check_vma=False,
    )
```

```python
import functools
import math

import jax
import jax.numpy as jnp
from jax import lax
from jax.experimental import pallas as pl
from jax.experimental.pallas import tpu as pltpu
from jax.sharding import PartitionSpec as P

F32 = jnp.float32
BF16 = jnp.bfloat16
LANES = 128
HALO = 4
MESH = pl.DeviceIdType.MESH
CONTRACT_LAST = (((1,), (1,)), ((), ()))


def split_bf16(value):
    high = value.astype(BF16)
    low = (value - high.astype(F32)).astype(BF16)
    return high, low


def remote(source, target, send, recv, peer):
    return pltpu.make_async_remote_copy(
        src_ref=source, dst_ref=target, send_sem=send, recv_sem=recv,
        device_id={"sky": peer}, device_id_type=MESH,
    )


def sweep_row(order, upper, middle, lower, older, link=None, field=None, split=None):
    channels, columns = middle.shape
    blocks = columns // LANES
    lane = lax.broadcasted_iota(jnp.int32, (channels, LANES), 1)
    sums = []
    for block in range(blocks):
        lanes = slice(block * LANES, (block + 1) * LANES)
        value = middle[:, lanes]
        if upper is not None:
            value = value + upper[:, lanes]
        if lower is not None:
            value = value + lower[:, lanes]
        sums.append(value)
    right_moved = [pltpu.roll(value, 1, 1) for value in sums]
    left_moved = [pltpu.roll(value, LANES - 1, 1) for value in sums]
    for block in range(blocks):
        lanes = slice(block * LANES, (block + 1) * LANES)
        from_left = jnp.where(lane == 0, right_moved[block - 1] if block > 0 else 0.0, right_moved[block])
        from_right = jnp.where(
            lane == LANES - 1, left_moved[block + 1] if block < blocks - 1 else 0.0, left_moved[block]
        )
        total = sums[block] + from_left + from_right - middle[:, lanes]
        if link is not None:
            total = total + link[:, lanes]
        if order == 1:
            result = -0.125 * total
        else:
            result = -0.25 * total - older[:, lanes]
        if field is not None:
            field[:, lanes] = result
        if split is not None:
            high, low = split_bf16(result)
            split[channels * order : channels * (order + 1), lanes] = high
            start = channels * (HALO + order)
            split[start : start + channels, lanes] = low


def stacked_weights(weights):
    orders = weights.shape[0]
    return jnp.concatenate(
        [weights[k] for k in range(orders)] + [weights[k] for k in range(1, orders)], axis=1
    )


def block_list(table, homes, slots, which):
    blocks = table.shape[-1] // LANES
    for entry in range(3):
        for block in range(blocks):
            homes[entry, block : block + 1, :] = jnp.right_shift(
                table[entry, :, block * LANES : (block + 1) * LANES], 7
            )
    lane = lax.broadcasted_iota(jnp.int32, (blocks, LANES), 1)
    packed = jnp.zeros((blocks, LANES), jnp.int32)
    more = jnp.zeros((blocks, 1), jnp.int32)
    for entry in range(3):
        home = homes[entry]
        first = jnp.min(home, axis=1, keepdims=True)
        second = jnp.min(jnp.where(home > first, home, blocks), axis=1, keepdims=True)
        third = jnp.min(jnp.where(home > second, home, blocks), axis=1, keepdims=True)
        packed = jnp.where(lane == entry, jnp.minimum(first, blocks - 1), packed)
        packed = jnp.where(lane == 3 + entry, jnp.minimum(second, blocks - 1), packed)
        more = jnp.maximum(more, (third < blocks).astype(jnp.int32))
    slots[which] = jnp.where(lane == 6, jnp.max(more, axis=0, keepdims=True), packed)


def exchange_kernel(
    sky,
    saved_hbm, scales_hbm, grad_hbm, weights_hbm, up_hbm, down_hbm,
    fields, split, acts, sums, slots, tables, left,
    saved, scales, grad, weights, flat, rows_x, scale_rows, homes,
    halo_send, halo_recv, table_send, table_recv, load,
):
    channels, rows, columns = saved.shape
    orders = weights.shape[0]
    blocks = scales.shape[2]
    width = columns // blocks
    me = lax.axis_index("sky")
    before = lax.rem(me + sky - 1, sky)
    after = lax.rem(me + 1, sky)

    barrier = pltpu.get_barrier_semaphore()
    for peer in (before, after):
        pl.semaphore_signal(barrier, inc=1, device_id={"sky": peer}, device_id_type=MESH)
    loads = [
        pltpu.make_async_copy(source, target, load.at[i])
        for i, (source, target) in enumerate(
            [
                (grad_hbm, grad),
                (up_hbm, tables.at[0]),
                (down_hbm, tables.at[1]),
                (saved_hbm, saved),
                (scales_hbm, scales),
                (weights_hbm, weights),
            ]
        )
    ]
    for copy in loads:
        copy.start()

    loads[0].wait()
    for channel in range(channels):
        flat[channel] = grad[channel].astype(F32)
    edge_first = [r for i in range(HALO) for r in (rows - 1 - i, i)]
    for r in edge_first:
        fields[0, HALO + r] = flat[:, r, :]
    loads[1].wait()
    loads[2].wait()
    pl.semaphore_wait(barrier, 2)

    copies = []
    for i in range(HALO):
        copies += [
            remote(fields.at[0, HALO + i], fields.at[0, HALO + rows + i], halo_send.at[0, i], halo_recv.at[0, i], before),
            remote(fields.at[0, HALO + rows - 1 - i], fields.at[0, HALO - 1 - i], halo_send.at[1, i], halo_recv.at[1, i], after),
        ]
    copies += [
        remote(tables.at[0], tables.at[3], table_send.at[0], table_recv.at[0], before),
        remote(tables.at[1], tables.at[2], table_send.at[1], table_recv.at[1], after),
    ]
    for copy in copies:
        copy.start()

    for r in range(HALO, rows - HALO):
        fields[0, HALO + r] = flat[:, r, :]

    @pl.loop(0, rows)
    def _(r):
        split[r, 0:channels] = fields[0, HALO + r].astype(BF16)

    for order in range(1, orders):
        @pl.loop(order, rows - order, step=2)
        def _(start):
            for r in (start, start + 1):
                row = HALO + r
                sweep_row(
                    order, fields.at[order - 1, row - 1], fields.at[order - 1, row], fields.at[order - 1, row + 1],
                    fields.at[order - 2, row] if order > 1 else None,
                    field=fields.at[order, row] if order < orders - 1 else None, split=split.at[r],
                )

    for copy in loads[3:]:
        copy.wait()
    for channel in range(channels):
        flat[channel] = saved[channel].astype(F32)
    for r in range(rows):
        rows_x[r] = flat[:, r, :]
        scale_rows[r] = scales[:, r, :]

    @pl.loop(0, rows)
    def _(r):
        for block in range(blocks):
            lanes = slice(block * width, (block + 1) * width)
            high, low = split_bf16(rows_x[r, :, lanes] * scale_rows[r, :, block : block + 1])
            acts[r, 0:channels, lanes] = high
            acts[r, channels : 2 * channels, lanes] = low

    left[...] = stacked_weights(weights)
    sums[...] = jnp.zeros_like(sums)
    for r in range(HALO, rows - HALO):
        sums[...] += lax.dot_general(acts[r], split[r], CONTRACT_LAST, preferred_element_type=F32)

    block_list(tables.at[0], homes, slots, 0)
    block_list(tables.at[1], homes, slots, 1)
    for copy in copies[2 * HALO :]:
        copy.wait()
    block_list(tables.at[2], homes, slots, 2)
    block_list(tables.at[3], homes, slots, 3)
    for copy in copies[: 2 * HALO]:
        copy.wait()


def linked_row(source, table, slots, which, target):
    channels, columns = source.shape
    blocks = columns // LANES

    def source_block(origin):
        return source[:, pl.ds(pl.multiple_of(origin * LANES, LANES), LANES)]

    def indices(entry, out_lanes):
        index = jnp.broadcast_to(table[entry, :, out_lanes], (channels, LANES))
        return jnp.right_shift(index, 7), jnp.bitwise_and(index, LANES - 1)

    def moved(values, lane):
        return jnp.take_along_axis(values, lane, axis=1, mode="promise_in_bounds")

    for block in range(blocks):
        out_lanes = slice(block * LANES, (block + 1) * LANES)
        total = None
        for entry in range(3):
            first, second = slots[which, block, entry], slots[which, block, 3 + entry]
            home, lane = indices(entry, out_lanes)
            picked = jnp.where(
                home == first,
                moved(source_block(first), lane),
                jnp.where(home == second, moved(source_block(second), lane), 0.0),
            )
            total = picked if total is None else total + picked
        target[:, out_lanes] = total

    @pl.when(slots[which, 0, 6] > 0)
    def _():
        @pl.loop(0, blocks)
        def _(block):
            out_lanes = pl.ds(pl.multiple_of(block * LANES, LANES), LANES)

            def add(origin, total):
                values = source_block(origin)
                for entry in range(3):
                    home, lane = indices(entry, out_lanes)
                    total = total + jnp.where(home == origin, moved(values, lane), 0.0)
                return total

            target[:, out_lanes] = lax.fori_loop(0, blocks, add, jnp.zeros((channels, LANES), F32))


def edge_kernel(fields, inner_split, slots, tables, split, fresh, links):
    rows = inner_split.shape[0]
    channels = fields.shape[2]
    orders = fields.shape[0] + 1
    top = HALO
    bottom = HALO + rows - 1
    mirror = 2 * HALO + rows - 1

    def field(order, row):
        if order == 0 or HALO + order <= row <= bottom - order:
            return fields.at[order, row]
        at = row - order if row <= HALO + order else HALO + row - (mirror - HALO - order + 1)
        return fresh.at[order - 1, at]

    def edge(r):
        return r if r < HALO else r - rows + 2 * HALO

    for r in range(HALO):
        for row in (r, rows - 1 - r):
            known = slice(0, channels * (r + 1))
            split[edge(row), known] = inner_split[row, known]
            if r > 0:
                known = slice(channels * (HALO + 1), channels * (HALO + 1 + r))
                split[edge(row), known] = inner_split[row, known]

    for order in range(1, orders):
        last = order == orders - 1
        linked_row(field(order - 1, top - 1), tables.at[0], slots, 0, links.at[0])
        linked_row(field(order - 1, bottom + 1), tables.at[1], slots, 1, links.at[1])
        if not last:
            linked_row(field(order - 1, top), tables.at[2], slots, 2, links.at[2])
            linked_row(field(order - 1, bottom), tables.at[3], slots, 3, links.at[3])
        for near in range(order, HALO + order):
            for row in (near, mirror - near):
                upper, lower, link = field(order - 1, row - 1), field(order - 1, row + 1), None
                if row == top:
                    upper, link = None, links.at[0]
                elif row == bottom:
                    lower, link = None, links.at[1]
                elif row == top - 1:
                    lower, link = None, links.at[2]
                elif row == bottom + 1:
                    upper, link = None, links.at[3]
                sweep_row(
                    order, upper, field(order - 1, row), lower, field(order - 2, row) if order > 1 else None,
                    link=link, field=None if last else field(order, row),
                    split=split.at[edge(row - HALO)] if top <= row <= bottom else None,
                )


def sum_kernel(
    sky, inner, norm,
    split, edge_split, acts, inner_sums, left,
    out, weight_grad,
    flat, part_in, part_out, in_send, in_recv, out_send, out_recv,
):
    channels, rows, columns = out.shape
    orders = weight_grad.shape[0]
    outer = sky // inner
    me = lax.axis_index("sky")
    slot = lax.rem(me, inner)
    group = lax.div(me, inner)

    def in_peer(step):
        return group * inner + lax.rem(slot + step, inner)

    def out_peer(step):
        return lax.rem(group + step, outer) * inner + slot

    barrier = pltpu.get_barrier_semaphore()
    peers = [in_peer(step) for step in range(1, inner)] + [out_peer(step) for step in range(1, outer)]
    for peer in peers:
        pl.semaphore_signal(barrier, inc=1, device_id={"sky": peer}, device_id_type=MESH)

    def terms(r):
        if r < HALO:
            return edge_split[r]
        return split[r] if r < rows - HALO else edge_split[r - rows + 2 * HALO]

    sums = inner_sums[...]
    for r in list(range(HALO)) + list(range(rows - HALO, rows)):
        sums += lax.dot_general(acts[r], terms(r), CONTRACT_LAST, preferred_element_type=F32)
    lane = lax.broadcasted_iota(jnp.int32, (channels, LANES), 1)
    both = sums[0:channels] + sums[channels : 2 * channels]
    first = both[:, 0:LANES]
    second = jnp.concatenate([both[:, LANES:], jnp.zeros((channels, 2 * LANES - both.shape[1]), F32)], axis=1)
    moved = jnp.where(lane < LANES // 2, pltpu.roll(first, LANES // 2, 1), pltpu.roll(second, LANES // 2, 1))
    wide = channels * orders
    part_in[slot] = jnp.where(lane < wide, first, 0.0) + jnp.where((lane >= channels) & (lane < wide), moved, 0.0)
    pl.semaphore_wait(barrier, len(peers))

    def exchange(buffer, own, count, peer_of, send, recv):
        copies = [
            remote(buffer.at[own], buffer.at[own], send.at[step], recv.at[step], peer_of(step))
            for step in range(1, count)
        ]
        for copy in copies:
            copy.start()
        return copies

    def total_of(buffer, copies):
        for copy in copies:
            copy.wait()
        return functools.reduce(lambda total, i: total + buffer[i], range(1, len(copies) + 1), buffer[0])

    copies = exchange(part_in, slot, inner, in_peer, in_send, in_recv)
    for r in range(rows):
        flat[:, r, :] = jnp.dot(left[...], terms(r), preferred_element_type=F32)
    part_out[group] = total_of(part_in, copies)
    copies = exchange(part_out, group, outer, out_peer, out_send, out_recv)
    for channel in range(channels):
        out[channel] = flat[channel].astype(BF16)
    total = total_of(part_out, copies) * norm
    for k in range(orders):
        weight_grad[k] = total[:, channels * k : channels * (k + 1)]


def on_device(sky, saved_acts, scales, grad_out, weights, edge_up, edge_down):
    channels, rows, columns = saved_acts.shape
    orders = weights.shape[0]
    blocks = scales.shape[2]
    inner = min(8, sky)
    outer = sky // inner
    norm = 1.0 / math.sqrt(rows * columns * sky)
    stacked = channels * (2 * orders - 1)
    vmem = pl.BlockSpec(memory_space=pltpu.VMEM)
    smem = pl.BlockSpec(memory_space=pltpu.SMEM)
    hbm = pl.BlockSpec(memory_space=pltpu.HBM)
    dma = pltpu.SemaphoreType.DMA
    shape = jax.ShapeDtypeStruct
    up, down = jnp.transpose(edge_up, (1, 0, 2)), jnp.transpose(edge_down, (1, 0, 2))
    fields, split, acts, sums, slots, tables, left = pl.pallas_call(
        functools.partial(exchange_kernel, sky),
        out_shape=(
            shape((orders - 1, rows + 2 * HALO, channels, columns), F32),
            shape((rows, stacked, columns), BF16),
            shape((rows, 2 * channels, columns), BF16),
            shape((2 * channels, stacked), F32),
            shape((4, columns // LANES, LANES), jnp.int32),
            shape((4, 3, 1, columns), jnp.int32),
            shape((channels, stacked), BF16),
        ),
        in_specs=[hbm] * 6,
        out_specs=(vmem,) * 7,
        scratch_shapes=[
            pltpu.VMEM((channels, rows, columns), BF16),
            pltpu.VMEM((channels, rows, blocks), F32),
            pltpu.VMEM((channels, rows, columns), BF16),
            pltpu.VMEM((orders, channels, channels), BF16),
            pltpu.VMEM((channels, rows, columns), F32),
            pltpu.VMEM((rows, channels, columns), F32),
            pltpu.VMEM((rows, channels, blocks), F32),
            pltpu.VMEM((3, columns // LANES, LANES), jnp.int32),
            dma((2, HALO)), dma((2, HALO)), dma((2,)), dma((2,)), dma((6,)),
        ],
        compiler_params=pltpu.CompilerParams(
            collective_id=0, has_side_effects=True, vmem_limit_bytes=12 * 2**20
        ),
        name="exchange",
    )(*(pltpu.with_memory_space_constraint(x, pltpu.HBM) for x in (saved_acts, scales, grad_out, weights, up, down)))
    edge_split = pl.pallas_call(
        edge_kernel,
        out_shape=shape((2 * HALO, stacked, columns), BF16),
        in_specs=[vmem, vmem, smem, vmem],
        out_specs=vmem,
        scratch_shapes=[
            pltpu.VMEM((orders - 2, 2 * HALO, channels, columns), F32),
            pltpu.VMEM((4, channels, columns), F32),
        ],
        compiler_params=pltpu.CompilerParams(vmem_limit_bytes=12 * 2**20),
        name="edges",
    )(fields, split, slots, tables)
    return pl.pallas_call(
        functools.partial(sum_kernel, sky, inner, norm),
        out_shape=(shape((channels, rows, columns), BF16), shape((orders, channels, channels), F32)),
        in_specs=[vmem] * 5,
        out_specs=(vmem, vmem),
        scratch_shapes=[
            pltpu.VMEM((channels, rows, columns), F32),
            pltpu.VMEM((inner, channels, LANES), F32),
            pltpu.VMEM((outer, channels, LANES), F32),
            dma((inner,)), dma((inner,)), dma((outer,)), dma((outer,)),
        ],
        compiler_params=pltpu.CompilerParams(
            collective_id=1, has_side_effects=True, vmem_limit_bytes=12 * 2**20
        ),
        name="sky_sum",
    )(split, edge_split, acts, sums, left)


def solution(mesh):
    return jax.shard_map(
        functools.partial(on_device, mesh.shape["sky"]),
        mesh=mesh,
        in_specs=(
            P("rep", "sky", None),
            P("rep", "sky", None),
            P("rep", "sky", None),
            P(),
            P("sky", None, None),
            P("sky", None, None),
        ),
        out_specs=(P("rep", "sky", None), P("rep", None, None)),
        check_vma=False,
    )
```

```python
import functools
import math

import jax
import jax.numpy as jnp
from jax import lax
from jax.experimental import pallas as pl
from jax.experimental.pallas import tpu as pltpu
from jax.sharding import PartitionSpec as P

F32 = jnp.float32
BF16 = jnp.bfloat16
LANES = 128
HALO = 4
MESH = pl.DeviceIdType.MESH
CONTRACT_LAST = (((1,), (1,)), ((), ()))
TERMS = ((0, 0), (1, 0), (2, 0), (2, 1), (3, 0), (3, 1), (4, 0), (4, 1))
LEVELS = 10922.0
GATHER = lax.GatherDimensionNumbers(
    offset_dims=(), collapsed_slice_dims=(1,), start_index_map=(1,),
    operand_batching_dims=(0,), start_indices_batching_dims=(0,),
)


def split_bf16(value):
    high = value.astype(BF16)
    low = (value - high.astype(F32)).astype(BF16)
    return high, low


def remote(source, target, send, recv, peer):
    return pltpu.make_async_remote_copy(
        src_ref=source, dst_ref=target, send_sem=send, recv_sem=recv,
        device_id={"sky": peer}, device_id_type=MESH,
    )


def sweep_row(order, upper, middle, lower, older, link=None, field=None, split=None):
    channels, columns = middle.shape
    blocks = columns // LANES
    lane = lax.broadcasted_iota(jnp.int32, (channels, LANES), 1)
    sums = []
    for block in range(blocks):
        lanes = slice(block * LANES, (block + 1) * LANES)
        value = middle[:, lanes]
        if upper is not None:
            value = value + upper[:, lanes]
        if lower is not None:
            value = value + lower[:, lanes]
        sums.append(value)
    right_moved = [pltpu.roll(value, 1, 1) for value in sums]
    left_moved = [pltpu.roll(value, LANES - 1, 1) for value in sums]
    for block in range(blocks):
        lanes = slice(block * LANES, (block + 1) * LANES)
        from_left = jnp.where(lane == 0, right_moved[block - 1] if block > 0 else 0.0, right_moved[block])
        from_right = jnp.where(
            lane == LANES - 1, left_moved[block + 1] if block < blocks - 1 else 0.0, left_moved[block]
        )
        total = sums[block] + from_left + from_right - middle[:, lanes]
        if link is not None:
            total = total + link[:, lanes]
        if order == 1:
            result = -0.125 * total
        else:
            result = -0.25 * total - older[:, lanes]
        if field is not None:
            field[:, lanes] = result
        if split is not None:
            start = channels * TERMS.index((order, 0))
            if order == 1:
                split[start : start + channels, lanes] = result.astype(BF16)
            else:
                high, low = split_bf16(result)
                split[start : start + channels, lanes] = high
                split[start + channels : start + 2 * channels, lanes] = low


def stacked_weights(weights):
    return jnp.concatenate([weights[k] for k, _ in TERMS], axis=1)


def block_list(table, homes, slots, which):
    blocks = table.shape[-1] // LANES
    for entry in range(3):
        for block in range(blocks):
            homes[entry, block : block + 1, :] = jnp.right_shift(
                table[entry, :, block * LANES : (block + 1) * LANES], 7
            )
    lane = lax.broadcasted_iota(jnp.int32, (blocks, LANES), 1)
    packed = jnp.zeros((blocks, LANES), jnp.int32)
    more = jnp.zeros((blocks, 1), jnp.int32)
    for entry in range(3):
        home = homes[entry]
        first = jnp.min(home, axis=1, keepdims=True)
        second = jnp.min(jnp.where(home > first, home, blocks), axis=1, keepdims=True)
        third = jnp.min(jnp.where(home > second, home, blocks), axis=1, keepdims=True)
        packed = jnp.where(lane == entry, jnp.minimum(first, blocks - 1), packed)
        packed = jnp.where(lane == 3 + entry, jnp.minimum(second, blocks - 1), packed)
        more = jnp.maximum(more, (third < blocks).astype(jnp.int32))
    slots[which] = jnp.where(lane == 6, jnp.max(more, axis=0, keepdims=True), packed)


def exchange_kernel(
    sky,
    saved_hbm, scales_hbm, grad_hbm, weights_hbm, up_hbm, down_hbm,
    fields, split, acts, sums, slots, tables, left,
    saved, scales, grad, weights, flat, rows_x, scale_rows, homes,
    halo_send, halo_recv, table_send, table_recv, load,
):
    channels, rows, columns = saved.shape
    orders = weights.shape[0]
    blocks = scales.shape[2]
    width = columns // blocks
    me = lax.axis_index("sky")
    before = lax.rem(me + sky - 1, sky)
    after = lax.rem(me + 1, sky)

    barrier = pltpu.get_barrier_semaphore()
    for peer in (before, after):
        pl.semaphore_signal(barrier, inc=1, device_id={"sky": peer}, device_id_type=MESH)
    loads = [
        pltpu.make_async_copy(source, target, load.at[i])
        for i, (source, target) in enumerate(
            [
                *((grad_hbm.at[pl.ds(4 * i, 4)], grad.at[pl.ds(4 * i, 4)]) for i in range(channels // 4)),
                (up_hbm, tables.at[0]),
                (down_hbm, tables.at[1]),
                (saved_hbm, saved),
                (scales_hbm, scales),
                (weights_hbm, weights),
            ]
        )
    ]
    for copy in loads:
        copy.start()

    chunks = channels // 4
    for channel in range(channels):
        if channel % 4 == 0:
            loads[channel // 4].wait()
        flat[channel] = grad[channel].astype(F32)
    edge_first = [r for i in range(HALO) for r in (rows - 1 - i, i)]
    for r in edge_first:
        fields[0, HALO + r] = flat[:, r, :]
    loads[chunks].wait()
    loads[chunks + 1].wait()
    pl.semaphore_wait(barrier, 2)

    copies = []
    for i in range(HALO):
        copies += [
            remote(fields.at[0, HALO + i], fields.at[0, HALO + rows + i], halo_send.at[0, i], halo_recv.at[0, i], before),
            remote(fields.at[0, HALO + rows - 1 - i], fields.at[0, HALO - 1 - i], halo_send.at[1, i], halo_recv.at[1, i], after),
        ]
    copies += [
        remote(tables.at[0], tables.at[3], table_send.at[0], table_recv.at[0], before),
        remote(tables.at[1], tables.at[2], table_send.at[1], table_recv.at[1], after),
    ]
    for copy in copies:
        copy.start()

    for r in range(HALO, rows - HALO):
        fields[0, HALO + r] = flat[:, r, :]

    @pl.loop(0, rows)
    def _(r):
        split[r, 0:channels] = fields[0, HALO + r].astype(BF16)

    for order in range(1, orders):
        @pl.loop(order, rows - order, step=2)
        def _(start):
            for r in (start, start + 1):
                row = HALO + r
                sweep_row(
                    order, fields.at[order - 1, row - 1], fields.at[order - 1, row], fields.at[order - 1, row + 1],
                    fields.at[order - 2, row] if order > 1 else None,
                    field=fields.at[order, row] if order < orders - 1 else None, split=split.at[r],
                )

    for copy in loads[chunks + 2 :]:
        copy.wait()
    for channel in range(channels):
        flat[channel] = saved[channel].astype(F32)
    for r in range(rows):
        rows_x[r] = flat[:, r, :]
        scale_rows[r] = scales[:, r, :]

    @pl.loop(0, rows)
    def _(r):
        for block in range(blocks):
            lanes = slice(block * width, (block + 1) * width)
            high, low = split_bf16(rows_x[r, :, lanes] * scale_rows[r, :, block : block + 1])
            acts[r, 0:channels, lanes] = high
            acts[r, channels : 2 * channels, lanes] = low

    left[...] = stacked_weights(weights)
    sums[...] = jnp.zeros_like(sums)
    for r in range(HALO, rows - HALO):
        sums[...] += lax.dot_general(acts[r], split[r], CONTRACT_LAST, preferred_element_type=F32)

    block_list(tables.at[0], homes, slots, 0)
    block_list(tables.at[1], homes, slots, 1)
    for copy in copies[2 * HALO :]:
        copy.wait()
    block_list(tables.at[2], homes, slots, 2)
    block_list(tables.at[3], homes, slots, 3)
    for copy in copies[: 2 * HALO]:
        copy.wait()


def pack_row(source, packed):
    value = source[...]
    half = value.shape[0] // 2
    peak = jnp.maximum(jnp.max(jnp.abs(value), axis=1, keepdims=True), 1e-30)
    level = jnp.round(value * (LEVELS / peak)).astype(jnp.int32)
    packed[...] = level[:half] * 65536 + level[half:]
    return peak * (1.0 / LEVELS)


def unpack(total, step):
    half = total.shape[0]
    second = jnp.right_shift(jnp.left_shift(total, 16), 16)
    first = jnp.right_shift(total - second, 16)
    return first.astype(F32) * step[:half], second.astype(F32) * step[half:]


def linked_rows(jobs, tables, slots, packed, links):
    half, columns = packed.shape[1:]
    blocks = columns // LANES

    def source_block(which, origin):
        return packed[which, :, pl.ds(pl.multiple_of(origin * LANES, LANES), LANES)]

    def indices(which, entry, out_lanes):
        index = jnp.broadcast_to(tables[which, entry, :, out_lanes], (half, LANES))
        return jnp.right_shift(index, 7), jnp.bitwise_and(index, LANES - 1)

    def moved(values, lane):
        return lax.gather(
            values, lane[..., None], GATHER, (1, 1), mode=lax.GatherScatterMode.PROMISE_IN_BOUNDS
        )

    def put(which, out_lanes, total, step):
        first, second = unpack(total, step)
        links[which, 0:half, out_lanes] = first
        links[which, half : 2 * half, out_lanes] = second

    steps = {which: pack_row(source, packed.at[which]) for source, which in jobs}
    for block in range(blocks):
        out_lanes = slice(block * LANES, (block + 1) * LANES)
        for _, which in jobs:
            total = None
            for entry in range(3):
                first, second = slots[which, block, entry], slots[which, block, 3 + entry]
                home, lane = indices(which, entry, out_lanes)
                picked = jnp.where(
                    home == first,
                    moved(source_block(which, first), lane),
                    jnp.where(home == second, moved(source_block(which, second), lane), 0),
                )
                total = picked if total is None else total + picked
            put(which, out_lanes, total, steps[which])

    for _, which in jobs:
        @pl.when(slots[which, 0, 6] > 0)
        def _():
            @pl.loop(0, blocks)
            def _(block):
                out_lanes = pl.ds(pl.multiple_of(block * LANES, LANES), LANES)

                def add(origin, total):
                    values = source_block(which, origin)
                    for entry in range(3):
                        home, lane = indices(which, entry, out_lanes)
                        total = total + jnp.where(home == origin, moved(values, lane), 0)
                    return total

                total = lax.fori_loop(0, blocks, add, jnp.zeros((half, LANES), jnp.int32))
                put(which, out_lanes, total, steps[which])


def edge_kernel(fields, inner_split, slots, tables, split, second, third, last_links, fresh, links, packed):
    rows = inner_split.shape[0]
    channels = fields.shape[2]
    orders = fields.shape[0] + 1
    top = HALO
    bottom = HALO + rows - 1
    mirror = 2 * HALO + rows - 1

    def field(order, row):
        if order == 0 or HALO + order <= row <= bottom - order:
            return fields.at[order, row]
        side, depth = (0, row - HALO) if row <= HALO + order else (1, bottom - row)
        if depth >= 0 and order == orders - 3:
            return second.at[side, depth]
        if depth >= 0 and order == orders - 2:
            return third.at[side, depth]
        return fresh.at[order - 1, side, depth + HALO - order]

    def edge(r):
        return r if r < HALO else r - rows + 2 * HALO

    for r in range(HALO):
        known = slice(0, channels * TERMS.index((r + 1, 0)))
        for row in (r, rows - 1 - r):
            split[edge(row), known] = inner_split[row, known]
    for depth in range(HALO + 1):
        for side, row in ((0, top + depth), (1, bottom - depth)):
            if orders - 3 <= depth < HALO:
                second[side, depth] = fields[orders - 3, row]
            if depth >= orders - 2:
                third[side, depth] = fields[orders - 2, row]

    for order in range(1, orders):
        last = order == orders - 1
        jobs = [(field(order - 1, top - 1), 0), (field(order - 1, bottom + 1), 1)]
        if last:
            linked_rows(jobs, tables, slots, packed, last_links)
            break
        jobs += [(field(order - 1, top), 2), (field(order - 1, bottom), 3)]
        linked_rows(jobs, tables, slots, packed, links)
        for near in range(order, HALO + order):
            for row in (near, mirror - near):
                upper, lower, link = field(order - 1, row - 1), field(order - 1, row + 1), None
                if row == top:
                    upper, link = None, links.at[0]
                elif row == bottom:
                    lower, link = None, links.at[1]
                elif row == top - 1:
                    lower, link = None, links.at[2]
                elif row == bottom + 1:
                    upper, link = None, links.at[3]
                sweep_row(
                    order, upper, field(order - 1, row), lower, field(order - 2, row) if order > 1 else None,
                    link=link, field=field(order, row),
                    split=split.at[edge(row - HALO)] if top <= row <= bottom else None,
                )


def sum_kernel(
    sky, inner,
    split, edge_split, second, third, last_links, acts, inner_sums, left,
    flat, total,
    full, part_in, part_out, in_send, in_recv, out_send, out_recv,
):
    rows, stacked, columns = split.shape
    known = edge_split.shape[1]
    orders = third.shape[1]
    outer = sky // inner
    me = lax.axis_index("sky")
    slot = lax.rem(me, inner)
    group = lax.div(me, inner)

    def in_peer(step):
        return group * inner + lax.rem(slot + step, inner)

    def out_peer(step):
        return lax.rem(group + step, outer) * inner + slot

    barrier = pltpu.get_barrier_semaphore()
    peers = [in_peer(step) for step in range(1, inner)] + [out_peer(step) for step in range(1, outer)]
    for peer in peers:
        pl.semaphore_signal(barrier, inc=1, device_id={"sky": peer}, device_id_type=MESH)

    full[:, 0:known] = edge_split[...]
    for side in range(2):
        def edge(depth):
            return full.at[depth if side == 0 else 2 * HALO - 1 - depth]

        sweep_row(
            orders - 1, None, third.at[side, 0], third.at[side, 1], second.at[side, 0],
            link=last_links.at[side], split=edge(0),
        )

        @pl.loop(1, HALO)
        def _(depth):
            sweep_row(
                orders - 1, third.at[side, depth - 1], third.at[side, depth], third.at[side, depth + 1],
                second.at[side, depth], split=edge(depth),
            )

    def edge_rows():
        return [(r, r) for r in range(HALO)] + [(rows - 2 * HALO + r, r) for r in range(HALO, 2 * HALO)]

    sums = inner_sums[...]
    for r, at in edge_rows():
        sums += lax.dot_general(acts[r], full[at], CONTRACT_LAST, preferred_element_type=F32)
    channels = sums.shape[0] // 2
    part_in[slot] = sums[0:channels] + sums[channels : 2 * channels]
    pl.semaphore_wait(barrier, len(peers))

    def exchange(buffer, own, count, peer_of, send, recv):
        copies = [
            remote(buffer.at[own], buffer.at[own], send.at[step], recv.at[step], peer_of(step))
            for step in range(1, count)
        ]
        for copy in copies:
            copy.start()
        return copies

    def total_of(buffer, copies):
        for copy in copies:
            copy.wait()
        return functools.reduce(lambda total, i: total + buffer[i], range(1, len(copies) + 1), buffer[0])

    copies = exchange(part_in, slot, inner, in_peer, in_send, in_recv)
    for r, at in edge_rows():
        flat[:, r, :] = jnp.dot(left[...], full[at], preferred_element_type=F32)
    part_out[group] = total_of(part_in, copies)
    copies = exchange(part_out, group, outer, out_peer, out_send, out_recv)
    for r in range(HALO, rows - HALO):
        flat[:, r, :] = jnp.dot(left[...], split[r], preferred_element_type=F32)
    total[...] = total_of(part_out, copies)


def result_kernel(norm, flat, total, out, weight_grad):
    channels = out.shape[0]
    for channel in range(channels):
        out[channel] = flat[channel].astype(BF16)
    scaled = total[...] * norm
    for k in range(weight_grad.shape[0]):
        parts = [scaled[:, channels * i : channels * (i + 1)] for i, (order, _) in enumerate(TERMS) if order == k]
        weight_grad[k] = functools.reduce(jnp.add, parts)


def on_device(sky, saved_acts, scales, grad_out, weights, edge_up, edge_down):
    channels, rows, columns = saved_acts.shape
    orders = weights.shape[0]
    blocks = scales.shape[2]
    inner = min(8, sky)
    outer = sky // inner
    norm = 1.0 / math.sqrt(rows * columns * sky)
    stacked = channels * len(TERMS)
    known = channels * TERMS.index((orders - 1, 0))
    edge = 2 * HALO
    vmem = pl.BlockSpec(memory_space=pltpu.VMEM)
    smem = pl.BlockSpec(memory_space=pltpu.SMEM)
    hbm = pl.BlockSpec(memory_space=pltpu.HBM)
    dma = pltpu.SemaphoreType.DMA
    shape = jax.ShapeDtypeStruct
    up, down = jnp.transpose(edge_up, (1, 0, 2)), jnp.transpose(edge_down, (1, 0, 2))
    fields, split, acts, sums, slots, tables, left = pl.pallas_call(
        functools.partial(exchange_kernel, sky),
        out_shape=(
            shape((orders - 1, rows + 2 * HALO, channels, columns), F32),
            shape((rows, stacked, columns), BF16),
            shape((rows, 2 * channels, columns), BF16),
            shape((2 * channels, stacked), F32),
            shape((4, columns // LANES, LANES), jnp.int32),
            shape((4, 3, 1, columns), jnp.int32),
            shape((channels, stacked), BF16),
        ),
        in_specs=[hbm] * 6,
        out_specs=(vmem,) * 7,
        scratch_shapes=[
            pltpu.VMEM((channels, rows, columns), BF16),
            pltpu.VMEM((channels, rows, blocks), F32),
            pltpu.VMEM((channels, rows, columns), BF16),
            pltpu.VMEM((orders, channels, channels), BF16),
            pltpu.VMEM((channels, rows, columns), F32),
            pltpu.VMEM((rows, channels, columns), F32),
            pltpu.VMEM((rows, channels, blocks), F32),
            pltpu.VMEM((3, columns // LANES, LANES), jnp.int32),
            dma((2, HALO)), dma((2, HALO)), dma((2,)), dma((2,)), dma((channels // 4 + 5,)),
        ],
        compiler_params=pltpu.CompilerParams(
            collective_id=0, has_side_effects=True, vmem_limit_bytes=12 * 2**20
        ),
        name="exchange",
    )(*(pltpu.with_memory_space_constraint(x, pltpu.HBM) for x in (saved_acts, scales, grad_out, weights, up, down)))
    edge_split, second, third, last_links = pl.pallas_call(
        edge_kernel,
        out_shape=(
            shape((edge, known, columns), BF16),
            shape((2, HALO, channels, columns), F32),
            shape((2, HALO + 1, channels, columns), F32),
            shape((2, channels, columns), F32),
        ),
        in_specs=[vmem, vmem, smem, vmem],
        out_specs=(vmem,) * 4,
        scratch_shapes=[
            pltpu.VMEM((orders - 2, 2, HALO + 1, channels, columns), F32),
            pltpu.VMEM((4, channels, columns), F32),
            pltpu.VMEM((4, channels // 2, columns), jnp.int32),
        ],
        compiler_params=pltpu.CompilerParams(vmem_limit_bytes=12 * 2**20),
        name="edges",
    )(fields, split, slots, tables)
    flat, total = pl.pallas_call(
        functools.partial(sum_kernel, sky, inner),
        out_shape=(shape((channels, rows, columns), F32), shape((channels, stacked), F32)),
        in_specs=[vmem] * 8,
        out_specs=(vmem, vmem),
        scratch_shapes=[
            pltpu.VMEM((edge, stacked, columns), BF16),
            pltpu.VMEM((inner, channels, stacked), F32),
            pltpu.VMEM((outer, channels, stacked), F32),
            dma((inner,)), dma((inner,)), dma((outer,)), dma((outer,)),
        ],
        compiler_params=pltpu.CompilerParams(
            collective_id=1, has_side_effects=True, vmem_limit_bytes=12 * 2**20
        ),
        name="sky_sum",
    )(split, edge_split, second, third, last_links, acts, sums, left)
    return pl.pallas_call(
        functools.partial(result_kernel, norm),
        out_shape=(shape((channels, rows, columns), BF16), shape((orders, channels, channels), F32)),
        in_specs=[vmem] * 2,
        out_specs=(vmem, vmem),
        compiler_params=pltpu.CompilerParams(vmem_limit_bytes=12 * 2**20),
        name="results",
    )(flat, total)


def solution(mesh):
    return jax.shard_map(
        functools.partial(on_device, mesh.shape["sky"]),
        mesh=mesh,
        in_specs=(
            P("rep", "sky", None),
            P("rep", "sky", None),
            P("rep", "sky", None),
            P(),
            P("sky", None, None),
            P("sky", None, None),
        ),
        out_specs=(P("rep", "sky", None), P("rep", None, None)),
        check_vma=False,
    )
```

```python
import functools
import math

import jax
import jax.numpy as jnp
from jax import lax
from jax.experimental import pallas as pl
from jax.experimental.pallas import tpu as pltpu
from jax.sharding import PartitionSpec as P

F32 = jnp.float32
BF16 = jnp.bfloat16
LANES = 128
HALO = 4
MESH = pl.DeviceIdType.MESH
CONTRACT_LAST = (((1,), (1,)), ((), ()))
TERMS = ((0, 0), (1, 0), (2, 0), (2, 1), (3, 0), (3, 1), (4, 0), (4, 1))
LEVELS = 10922.0
GATHER = lax.GatherDimensionNumbers(
    offset_dims=(), collapsed_slice_dims=(1,), start_index_map=(1,),
    operand_batching_dims=(0,), start_indices_batching_dims=(0,),
)


def split_bf16(value):
    high = value.astype(BF16)
    low = (value - high.astype(F32)).astype(BF16)
    return high, low


def remote(source, target, send, recv, peer):
    return pltpu.make_async_remote_copy(
        src_ref=source, dst_ref=target, send_sem=send, recv_sem=recv,
        device_id={"sky": peer}, device_id_type=MESH,
    )


def sweep_row(order, upper, middle, lower, older, link=None, field=None, split=None):
    channels, columns = middle.shape
    blocks = columns // LANES
    lane = lax.broadcasted_iota(jnp.int32, (channels, LANES), 1)
    sums = []
    for block in range(blocks):
        lanes = slice(block * LANES, (block + 1) * LANES)
        value = middle[:, lanes]
        if upper is not None:
            value = value + upper[:, lanes]
        if lower is not None:
            value = value + lower[:, lanes]
        sums.append(value)
    right_moved = [pltpu.roll(value, 1, 1) for value in sums]
    left_moved = [pltpu.roll(value, LANES - 1, 1) for value in sums]
    for block in range(blocks):
        lanes = slice(block * LANES, (block + 1) * LANES)
        from_left = jnp.where(lane == 0, right_moved[block - 1] if block > 0 else 0.0, right_moved[block])
        from_right = jnp.where(
            lane == LANES - 1, left_moved[block + 1] if block < blocks - 1 else 0.0, left_moved[block]
        )
        total = sums[block] + from_left + from_right - middle[:, lanes]
        if link is not None:
            total = total + link[:, lanes]
        if order == 1:
            result = -0.125 * total
        else:
            result = -0.25 * total - older[:, lanes]
        if field is not None:
            field[:, lanes] = result
        if split is not None:
            start = channels * TERMS.index((order, 0))
            if order == 1:
                split[start : start + channels, lanes] = result.astype(BF16)
            else:
                high, low = split_bf16(result)
                split[start : start + channels, lanes] = high
                split[start + channels : start + 2 * channels, lanes] = low


def stacked_weights(weights):
    return jnp.concatenate([weights[k] for k, _ in TERMS], axis=1)


def block_list(table, arranged, codes, slots, which):
    blocks = table.shape[-1] // LANES
    for entry in range(3):
        for block in range(blocks):
            arranged[entry, block : block + 1, :] = table[entry, :, block * LANES : (block + 1) * LANES]
    lane = lax.broadcasted_iota(jnp.int32, (blocks, LANES), 1)
    packed = jnp.zeros((blocks, LANES), jnp.int32)
    more = jnp.zeros((blocks, 1), jnp.int32)
    for entry in range(3):
        index = arranged[entry]
        home = jnp.right_shift(index, 7)
        first = jnp.min(home, axis=1, keepdims=True)
        second = jnp.min(jnp.where(home > first, home, blocks), axis=1, keepdims=True)
        third = jnp.min(jnp.where(home > second, home, blocks), axis=1, keepdims=True)
        first = jnp.minimum(first, blocks - 1)
        second = jnp.minimum(second, blocks - 1)
        slot = jnp.where(home == first, 0, jnp.where(home == second, LANES, 2 * LANES))
        codes[which, entry] = jnp.bitwise_and(index, LANES - 1) + slot
        packed = jnp.where(lane == entry, first, packed)
        packed = jnp.where(lane == 3 + entry, second, packed)
        more = jnp.maximum(more, (third < blocks).astype(jnp.int32))
    slots[which] = jnp.where(lane == 6, jnp.max(more, axis=0, keepdims=True), packed)


def exchange_kernel(
    sky,
    saved_hbm, scales_hbm, grad_hbm, weights_hbm, up_hbm, down_hbm,
    fields, split, acts, slots, codes, tables, left,
    saved, scales, grad, weights, flat, rows_x, scale_rows, arranged,
    halo_send, halo_recv, table_send, table_recv, load,
):
    channels, rows, columns = saved.shape
    orders = weights.shape[0]
    blocks = scales.shape[2]
    width = columns // blocks
    me = lax.axis_index("sky")
    before = lax.rem(me + sky - 1, sky)
    after = lax.rem(me + 1, sky)

    barrier = pltpu.get_barrier_semaphore()
    for peer in (before, after):
        pl.semaphore_signal(barrier, inc=1, device_id={"sky": peer}, device_id_type=MESH)
    loads = [
        pltpu.make_async_copy(source, target, load.at[i])
        for i, (source, target) in enumerate(
            [
                *((grad_hbm.at[pl.ds(4 * i, 4)], grad.at[pl.ds(4 * i, 4)]) for i in range(channels // 4)),
                (up_hbm, tables.at[0]),
                (down_hbm, tables.at[1]),
                (saved_hbm, saved),
                (scales_hbm, scales),
                (weights_hbm, weights),
            ]
        )
    ]
    for copy in loads:
        copy.start()

    chunks = channels // 4
    for channel in range(channels):
        if channel % 4 == 0:
            loads[channel // 4].wait()
        flat[channel] = grad[channel].astype(F32)
    edge_first = [r for i in range(HALO) for r in (rows - 1 - i, i)]
    for r in edge_first:
        fields[0, HALO + r] = flat[:, r, :]
    loads[chunks].wait()
    loads[chunks + 1].wait()
    pl.semaphore_wait(barrier, 2)

    copies = [
        remote(tables.at[0], tables.at[3], table_send.at[0], table_recv.at[0], before),
        remote(tables.at[1], tables.at[2], table_send.at[1], table_recv.at[1], after),
    ]
    for i in range(HALO):
        copies += [
            remote(fields.at[0, HALO + i], fields.at[0, HALO + rows + i], halo_send.at[0, i], halo_recv.at[0, i], before),
            remote(fields.at[0, HALO + rows - 1 - i], fields.at[0, HALO - 1 - i], halo_send.at[1, i], halo_recv.at[1, i], after),
        ]
    for copy in copies:
        copy.start()

    for r in range(HALO, rows - HALO):
        fields[0, HALO + r] = flat[:, r, :]

    @pl.loop(0, rows)
    def _(r):
        split[r, 0:channels] = fields[0, HALO + r].astype(BF16)

    for order in range(1, orders):
        @pl.loop(order, rows - order, step=2)
        def _(start):
            for r in (start, start + 1):
                row = HALO + r
                sweep_row(
                    order, fields.at[order - 1, row - 1], fields.at[order - 1, row], fields.at[order - 1, row + 1],
                    fields.at[order - 2, row] if order > 1 else None,
                    field=fields.at[order, row] if order < orders - 1 else None, split=split.at[r],
                )

    for copy in loads[chunks + 2 :]:
        copy.wait()
    for channel in range(channels):
        flat[channel] = saved[channel].astype(F32)
    for r in range(rows):
        rows_x[r] = flat[:, r, :]
        scale_rows[r] = scales[:, r, :]

    @pl.loop(0, rows)
    def _(r):
        for block in range(blocks):
            lanes = slice(block * width, (block + 1) * width)
            high, low = split_bf16(rows_x[r, :, lanes] * scale_rows[r, :, block : block + 1])
            acts[r, 0:channels, lanes] = high
            acts[r, channels : 2 * channels, lanes] = low

    left[...] = stacked_weights(weights)
    block_list(tables.at[0], arranged, codes, slots, 0)
    block_list(tables.at[1], arranged, codes, slots, 1)
    for copy in copies[:2]:
        copy.wait()
    block_list(tables.at[2], arranged, codes, slots, 2)
    block_list(tables.at[3], arranged, codes, slots, 3)
    for copy in copies[2:]:
        copy.wait()


def pack_row(source, packed):
    value = source[...]
    half = value.shape[0] // 2
    peak = jnp.maximum(jnp.max(jnp.abs(value), axis=1, keepdims=True), 1e-30)
    level = jnp.round(value * (LEVELS / peak)).astype(jnp.int32)
    both = level[:half] * 65536 + level[half:]
    for block in range(packed.shape[0]):
        packed[block] = both[:, block * LANES : (block + 1) * LANES]
    return peak * (1.0 / LEVELS)


def unpack(total, step):
    half = total.shape[0]
    second = jnp.right_shift(jnp.left_shift(total, 16), 16)
    first = jnp.right_shift(total - second, 16)
    return first.astype(F32) * step[:half], second.astype(F32) * step[half:]


def linked_rows(jobs, tables, codes, slots, packed, links):
    blocks, half = packed.shape[1:3]

    def moved(values, lane):
        return lax.gather(
            values, lane[..., None], GATHER, (1, 1), mode=lax.GatherScatterMode.PROMISE_IN_BOUNDS
        )

    def put(which, out_lanes, total, step):
        first, second = unpack(total, step)
        links[which, 0:half, out_lanes] = first
        links[which, half : 2 * half, out_lanes] = second

    steps = {which: pack_row(source, packed.at[which]) for source, which in jobs}
    for block in range(blocks):
        out_lanes = slice(block * LANES, (block + 1) * LANES)
        for _, which in jobs:
            total = None
            for entry in range(3):
                first, second = slots[which, block, entry], slots[which, block, 3 + entry]
                code = jnp.broadcast_to(codes[which, entry, block : block + 1, :], (half, LANES))
                lane = jnp.bitwise_and(code, LANES - 1)
                picked = jnp.where(
                    code < LANES,
                    moved(packed[which, first], lane),
                    jnp.where(code < 2 * LANES, moved(packed[which, second], lane), 0),
                )
                total = picked if total is None else total + picked
            put(which, out_lanes, total, steps[which])

    for _, which in jobs:
        @pl.when(slots[which, 0, 6] > 0)
        def _():
            @pl.loop(0, blocks)
            def _(block):
                out_lanes = pl.ds(pl.multiple_of(block * LANES, LANES), LANES)

                def add(origin, total):
                    values = packed[which, origin]
                    for entry in range(3):
                        index = jnp.broadcast_to(tables[which, entry, :, out_lanes], (half, LANES))
                        arrived = moved(values, jnp.bitwise_and(index, LANES - 1))
                        total = total + jnp.where(jnp.right_shift(index, 7) == origin, arrived, 0)
                    return total

                total = lax.fori_loop(0, blocks, add, jnp.zeros((half, LANES), jnp.int32))
                put(which, out_lanes, total, steps[which])


def edge_kernel(rows, fields, slots, codes, tables, split, second, third, last_links, fresh, links, packed):
    channels = fields.shape[2]
    orders = fields.shape[0] + 1
    top = HALO
    bottom = HALO + rows - 1
    mirror = 2 * HALO + rows - 1

    def field(order, row):
        if order == 0 or HALO + order <= row <= bottom - order:
            return fields.at[order, row]
        side, depth = (0, row - HALO) if row <= HALO + order else (1, bottom - row)
        if depth >= 0 and order == orders - 3:
            return second.at[side, depth]
        if depth >= 0 and order == orders - 2:
            return third.at[side, depth]
        return fresh.at[order - 1, side, depth + HALO - order]

    def edge(r):
        return r if r < HALO else r - rows + 2 * HALO

    for order in range(1, orders):
        last = order == orders - 1
        jobs = [(field(order - 1, top - 1), 0), (field(order - 1, bottom + 1), 1)]
        if last:
            linked_rows(jobs, tables, codes, slots, packed, last_links)
            break
        jobs += [(field(order - 1, top), 2), (field(order - 1, bottom), 3)]
        linked_rows(jobs, tables, codes, slots, packed, links)
        for near in range(order, HALO + order):
            for row in (near, mirror - near):
                upper, lower, link = field(order - 1, row - 1), field(order - 1, row + 1), None
                if row == top:
                    upper, link = None, links.at[0]
                elif row == bottom:
                    lower, link = None, links.at[1]
                elif row == top - 1:
                    lower, link = None, links.at[2]
                elif row == bottom + 1:
                    upper, link = None, links.at[3]
                sweep_row(
                    order, upper, field(order - 1, row), lower, field(order - 2, row) if order > 1 else None,
                    link=link, field=field(order, row),
                    split=split.at[edge(row - HALO)] if top <= row <= bottom else None,
                )


def sum_kernel(
    sky, inner,
    fields, split, edge_split, fresh_second, fresh_third, last_links, acts, left,
    flat, total,
    full, second, third, part_in, part_out, in_send, in_recv, out_send, out_recv,
):
    rows, stacked, columns = split.shape
    orders = HALO + 1
    channels = stacked // len(TERMS)
    outer = sky // inner
    me = lax.axis_index("sky")
    slot = lax.rem(me, inner)
    group = lax.div(me, inner)

    def in_peer(step):
        return group * inner + lax.rem(slot + step, inner)

    def out_peer(step):
        return lax.rem(group + step, outer) * inner + slot

    barrier = pltpu.get_barrier_semaphore()
    peers = [in_peer(step) for step in range(1, inner)] + [out_peer(step) for step in range(1, outer)]
    for peer in peers:
        pl.semaphore_signal(barrier, inc=1, device_id={"sky": peer}, device_id_type=MESH)

    for depth in range(HALO + 1):
        first = channels * TERMS.index((min(depth + 1, orders - 1), 0))
        known = channels * TERMS.index((orders - 1, 0))
        for side in range(2):
            row = depth if side == 0 else rows - 1 - depth
            if depth < HALO:
                at = depth if side == 0 else 2 * HALO - 1 - depth
                full[at, 0:first] = split[row, 0:first]
                if first < known:
                    full[at, first:known] = edge_split[at, first:known]
                old = depth >= orders - 3
                second[side, depth] = fields[orders - 3, HALO + row] if old else fresh_second[side, depth]
            old = depth >= orders - 2
            third[side, depth] = fields[orders - 2, HALO + row] if old else fresh_third[side, depth]

    for side in range(2):
        def edge(depth):
            return full.at[depth if side == 0 else 2 * HALO - 1 - depth]

        sweep_row(
            orders - 1, None, third.at[side, 0], third.at[side, 1], second.at[side, 0],
            link=last_links.at[side], split=edge(0),
        )

        @pl.loop(1, HALO)
        def _(depth):
            sweep_row(
                orders - 1, third.at[side, depth - 1], third.at[side, depth], third.at[side, depth + 1],
                second.at[side, depth], split=edge(depth),
            )

    def edge_rows():
        return [(r, r) for r in range(HALO)] + [(rows - 2 * HALO + r, r) for r in range(HALO, 2 * HALO)]

    sums = jnp.zeros((acts.shape[1], stacked), F32)
    for r in range(HALO, rows - HALO):
        sums += lax.dot_general(acts[r], split[r], CONTRACT_LAST, preferred_element_type=F32)
    for r, at in edge_rows():
        sums += lax.dot_general(acts[r], full[at], CONTRACT_LAST, preferred_element_type=F32)
    part_in[slot] = sums[0:channels] + sums[channels : 2 * channels]
    pl.semaphore_wait(barrier, len(peers))

    def exchange(buffer, own, count, peer_of, send, recv):
        copies = [
            remote(buffer.at[own], buffer.at[own], send.at[step], recv.at[step], peer_of(step))
            for step in range(1, count)
        ]
        for copy in copies:
            copy.start()
        return copies

    def total_of(buffer, copies):
        for copy in copies:
            copy.wait()
        return functools.reduce(lambda total, i: total + buffer[i], range(1, len(copies) + 1), buffer[0])

    copies = exchange(part_in, slot, inner, in_peer, in_send, in_recv)
    for r, at in edge_rows():
        flat[:, r, :] = jnp.dot(left[...], full[at], preferred_element_type=F32)
    part_out[group] = total_of(part_in, copies)
    copies = exchange(part_out, group, outer, out_peer, out_send, out_recv)
    for r in range(HALO, rows - HALO):
        flat[:, r, :] = jnp.dot(left[...], split[r], preferred_element_type=F32)
    total[...] = total_of(part_out, copies)


def result_kernel(norm, flat, total, out, weight_grad, rounded, store):
    channels = flat.shape[0]
    copies = []
    for start in range(0, channels, 4):
        for channel in range(start, start + 4):
            rounded[channel] = flat[channel].astype(BF16)
        part = pl.ds(start, 4)
        copies.append(pltpu.make_async_copy(rounded.at[part], out.at[part], store.at[start // 4]))
        copies[-1].start()
    scaled = total[...] * norm
    for k in range(weight_grad.shape[0]):
        parts = [scaled[:, channels * i : channels * (i + 1)] for i, (order, _) in enumerate(TERMS) if order == k]
        weight_grad[k] = functools.reduce(jnp.add, parts)
    for copy in copies:
        copy.wait()


def on_device(sky, saved_acts, scales, grad_out, weights, edge_up, edge_down):
    channels, rows, columns = saved_acts.shape
    orders = weights.shape[0]
    blocks = scales.shape[2]
    inner = min(8, sky)
    outer = sky // inner
    norm = 1.0 / math.sqrt(rows * columns * sky)
    stacked = channels * len(TERMS)
    known = channels * TERMS.index((orders - 1, 0))
    edge = 2 * HALO
    vmem = pl.BlockSpec(memory_space=pltpu.VMEM)
    smem = pl.BlockSpec(memory_space=pltpu.SMEM)
    hbm = pl.BlockSpec(memory_space=pltpu.HBM)
    dma = pltpu.SemaphoreType.DMA
    shape = jax.ShapeDtypeStruct
    up, down = jnp.transpose(edge_up, (1, 0, 2)), jnp.transpose(edge_down, (1, 0, 2))
    fields, split, acts, slots, codes, tables, left = pl.pallas_call(
        functools.partial(exchange_kernel, sky),
        out_shape=(
            shape((orders - 1, rows + 2 * HALO, channels, columns), F32),
            shape((rows, stacked, columns), BF16),
            shape((rows, 2 * channels, columns), BF16),
            shape((4, columns // LANES, LANES), jnp.int32),
            shape((4, 3, columns // LANES, LANES), jnp.int32),
            shape((4, 3, 1, columns), jnp.int32),
            shape((channels, stacked), BF16),
        ),
        in_specs=[hbm] * 6,
        out_specs=(vmem,) * 7,
        scratch_shapes=[
            pltpu.VMEM((channels, rows, columns), BF16),
            pltpu.VMEM((channels, rows, blocks), F32),
            pltpu.VMEM((channels, rows, columns), BF16),
            pltpu.VMEM((orders, channels, channels), BF16),
            pltpu.VMEM((channels, rows, columns), F32),
            pltpu.VMEM((rows, channels, columns), F32),
            pltpu.VMEM((rows, channels, blocks), F32),
            pltpu.VMEM((3, columns // LANES, LANES), jnp.int32),
            dma((2, HALO)), dma((2, HALO)), dma((2,)), dma((2,)), dma((channels // 4 + 5,)),
        ],
        compiler_params=pltpu.CompilerParams(
            collective_id=0, has_side_effects=True, vmem_limit_bytes=12 * 2**20
        ),
        name="exchange",
    )(*(pltpu.with_memory_space_constraint(x, pltpu.HBM) for x in (saved_acts, scales, grad_out, weights, up, down)))
    edge_split, second, third, last_links = pl.pallas_call(
        functools.partial(edge_kernel, rows),
        out_shape=(
            shape((edge, known, columns), BF16),
            shape((2, HALO - 2, channels, columns), F32),
            shape((2, HALO - 1, channels, columns), F32),
            shape((2, channels, columns), F32),
        ),
        in_specs=[vmem, smem, vmem, vmem],
        out_specs=(vmem,) * 4,
        scratch_shapes=[
            pltpu.VMEM((orders - 2, 2, HALO + 1, channels, columns), F32),
            pltpu.VMEM((4, channels, columns), F32),
            pltpu.VMEM((4, columns // LANES, channels // 2, LANES), jnp.int32),
        ],
        compiler_params=pltpu.CompilerParams(vmem_limit_bytes=12 * 2**20),
        name="edges",
    )(fields, slots, codes, tables)
    flat, total = pl.pallas_call(
        functools.partial(sum_kernel, sky, inner),
        out_shape=(shape((channels, rows, columns), F32), shape((channels, stacked), F32)),
        in_specs=[vmem] * 8,
        out_specs=(vmem, vmem),
        scratch_shapes=[
            pltpu.VMEM((edge, stacked, columns), BF16),
            pltpu.VMEM((2, HALO, channels, columns), F32),
            pltpu.VMEM((2, HALO + 1, channels, columns), F32),
            pltpu.VMEM((inner, channels, stacked), F32),
            pltpu.VMEM((outer, channels, stacked), F32),
            dma((inner,)), dma((inner,)), dma((outer,)), dma((outer,)),
        ],
        compiler_params=pltpu.CompilerParams(
            collective_id=1, has_side_effects=True, vmem_limit_bytes=12 * 2**20
        ),
        name="sky_sum",
    )(fields, split, edge_split, second, third, last_links, acts, left)
    return pl.pallas_call(
        functools.partial(result_kernel, norm),
        out_shape=(shape((channels, rows, columns), BF16), shape((orders, channels, channels), F32)),
        in_specs=[vmem] * 2,
        out_specs=(hbm, vmem),
        scratch_shapes=[pltpu.VMEM((channels, rows, columns), BF16), dma((channels // 4,))],
        compiler_params=pltpu.CompilerParams(vmem_limit_bytes=12 * 2**20),
        name="results",
    )(flat, total)


def solution(mesh):
    return jax.shard_map(
        functools.partial(on_device, mesh.shape["sky"]),
        mesh=mesh,
        in_specs=(
            P("rep", "sky", None),
            P("rep", "sky", None),
            P("rep", "sky", None),
            P(),
            P("sky", None, None),
            P("sky", None, None),
        ),
        out_specs=(P("rep", "sky", None), P("rep", None, None)),
        check_vma=False,
    )
```

```python
import functools
import math

import jax
import jax.numpy as jnp
from jax import lax
from jax.experimental import pallas as pl
from jax.experimental.pallas import tpu as pltpu
from jax.sharding import PartitionSpec as P

F32 = jnp.float32
BF16 = jnp.bfloat16
LANES = 128
HALO = 4
MESH = pl.DeviceIdType.MESH
CONTRACT_LAST = (((1,), (1,)), ((), ()))
TERMS = ((0, 0), (1, 0), (2, 0), (2, 1), (3, 0), (3, 1), (4, 0), (4, 1))
LEVELS = 10922.0
GATHER = lax.GatherDimensionNumbers(
    offset_dims=(), collapsed_slice_dims=(1,), start_index_map=(1,),
    operand_batching_dims=(0,), start_indices_batching_dims=(0,),
)


def split_bf16(value):
    high = value.astype(BF16)
    low = (value - high.astype(F32)).astype(BF16)
    return high, low


def remote(source, target, send, recv, peer):
    return pltpu.make_async_remote_copy(
        src_ref=source, dst_ref=target, send_sem=send, recv_sem=recv,
        device_id={"sky": peer}, device_id_type=MESH,
    )


def sweep_row(order, upper, middle, lower, older, link=None, field=None, split=None, start=None):
    channels, columns = middle.shape
    blocks = columns // LANES
    if start is None:
        start = channels * TERMS.index((order, 0))
    lane = lax.broadcasted_iota(jnp.int32, (channels, LANES), 1)
    sums = []
    for block in range(blocks):
        lanes = slice(block * LANES, (block + 1) * LANES)
        value = middle[:, lanes]
        if upper is not None:
            value = value + upper[:, lanes]
        if lower is not None:
            value = value + lower[:, lanes]
        sums.append(value)
    right_moved = [pltpu.roll(value, 1, 1) for value in sums]
    left_moved = [pltpu.roll(value, LANES - 1, 1) for value in sums]
    for block in range(blocks):
        lanes = slice(block * LANES, (block + 1) * LANES)
        from_left = jnp.where(lane == 0, right_moved[block - 1] if block > 0 else 0.0, right_moved[block])
        from_right = jnp.where(
            lane == LANES - 1, left_moved[block + 1] if block < blocks - 1 else 0.0, left_moved[block]
        )
        total = sums[block] + from_left + from_right - middle[:, lanes]
        if link is not None:
            total = total + link[:, lanes]
        if order == 1:
            result = -0.125 * total
        else:
            result = -0.25 * total - older[:, lanes]
        if field is not None:
            field[:, lanes] = result
        if split is not None:
            if order == 1:
                split[start : start + channels, lanes] = result.astype(BF16)
            else:
                high, low = split_bf16(result)
                split[start : start + channels, lanes] = high
                split[start + channels : start + 2 * channels, lanes] = low


def stacked_weights(weights):
    return jnp.concatenate([weights[k] for k, _ in TERMS], axis=1)


def block_list(table, arranged, codes, slots, which):
    blocks = table.shape[-1] // LANES
    for entry in range(3):
        for block in range(blocks):
            arranged[entry, block : block + 1, :] = table[entry, :, block * LANES : (block + 1) * LANES]
    lane = lax.broadcasted_iota(jnp.int32, (blocks, LANES), 1)
    packed = jnp.zeros((blocks, LANES), jnp.int32)
    more = jnp.zeros((blocks, 1), jnp.int32)
    for entry in range(3):
        index = arranged[entry]
        home = jnp.right_shift(index, 7)
        first = jnp.min(home, axis=1, keepdims=True)
        second = jnp.min(jnp.where(home > first, home, blocks), axis=1, keepdims=True)
        third = jnp.min(jnp.where(home > second, home, blocks), axis=1, keepdims=True)
        first = jnp.minimum(first, blocks - 1)
        second = jnp.minimum(second, blocks - 1)
        slot = jnp.where(home == first, 0, jnp.where(home == second, LANES, 2 * LANES))
        codes[which, entry] = jnp.bitwise_and(index, LANES - 1) + slot
        packed = jnp.where(lane == entry, first, packed)
        packed = jnp.where(lane == 3 + entry, second, packed)
        more = jnp.maximum(more, (third < blocks).astype(jnp.int32))
    slots[which] = jnp.where(lane == 6, jnp.max(more, axis=0, keepdims=True), packed)


def exchange_kernel(
    sky,
    saved_hbm, scales_hbm, grad_hbm, weights_hbm, up_hbm, down_hbm,
    fields, split, acts, sums, slots, codes, tables, left,
    saved, scales, grad, weights, flat, rows_x, scale_rows, arranged,
    halo_send, halo_recv, table_send, table_recv, load,
):
    channels, rows, columns = saved.shape
    orders = weights.shape[0]
    blocks = scales.shape[2]
    width = columns // blocks
    me = lax.axis_index("sky")
    before = lax.rem(me + sky - 1, sky)
    after = lax.rem(me + 1, sky)

    barrier = pltpu.get_barrier_semaphore()
    for peer in (before, after):
        pl.semaphore_signal(barrier, inc=1, device_id={"sky": peer}, device_id_type=MESH)
    loads = [
        pltpu.make_async_copy(source, target, load.at[i])
        for i, (source, target) in enumerate(
            [
                *((grad_hbm.at[pl.ds(4 * i, 4)], grad.at[pl.ds(4 * i, 4)]) for i in range(channels // 4)),
                (up_hbm, tables.at[0]),
                (down_hbm, tables.at[1]),
                (saved_hbm, saved),
                (scales_hbm, scales),
                (weights_hbm, weights),
            ]
        )
    ]
    for copy in loads:
        copy.start()

    chunks = channels // 4
    for channel in range(channels):
        if channel % 4 == 0:
            loads[channel // 4].wait()
        flat[channel] = grad[channel].astype(F32)
    edge_first = [r for i in range(HALO) for r in (rows - 1 - i, i)]
    for r in edge_first:
        fields[0, HALO + r] = flat[:, r, :]
    loads[chunks].wait()
    loads[chunks + 1].wait()
    pl.semaphore_wait(barrier, 2)

    copies = [
        remote(tables.at[0], tables.at[3], table_send.at[0], table_recv.at[0], before),
        remote(tables.at[1], tables.at[2], table_send.at[1], table_recv.at[1], after),
    ]
    for i in range(HALO):
        copies += [
            remote(fields.at[0, HALO + i], fields.at[0, HALO + rows + i], halo_send.at[0, i], halo_recv.at[0, i], before),
            remote(fields.at[0, HALO + rows - 1 - i], fields.at[0, HALO - 1 - i], halo_send.at[1, i], halo_recv.at[1, i], after),
        ]
    for copy in copies:
        copy.start()

    for r in range(HALO, rows - HALO):
        fields[0, HALO + r] = flat[:, r, :]

    @pl.loop(0, rows)
    def _(r):
        split[r, 0:channels] = fields[0, HALO + r].astype(BF16)

    for order in range(1, orders):
        @pl.loop(order, rows - order, step=2)
        def _(start):
            for r in (start, start + 1):
                row = HALO + r
                sweep_row(
                    order, fields.at[order - 1, row - 1], fields.at[order - 1, row], fields.at[order - 1, row + 1],
                    fields.at[order - 2, row] if order > 1 else None,
                    field=fields.at[order, row] if order < orders - 1 else None, split=split.at[r],
                )

    for copy in loads[chunks + 2 :]:
        copy.wait()
    for channel in range(channels):
        flat[channel] = saved[channel].astype(F32)
    for r in range(rows):
        rows_x[r] = flat[:, r, :]
        scale_rows[r] = scales[:, r, :]

    @pl.loop(0, rows)
    def _(r):
        for block in range(blocks):
            lanes = slice(block * width, (block + 1) * width)
            high, low = split_bf16(rows_x[r, :, lanes] * scale_rows[r, :, block : block + 1])
            acts[r, 0:channels, lanes] = high
            acts[r, channels : 2 * channels, lanes] = low

    left[...] = stacked_weights(weights)
    total = jnp.zeros(sums.shape, F32)
    for r in range(HALO, rows - HALO):
        total += lax.dot_general(acts[r], split[r], CONTRACT_LAST, preferred_element_type=F32)
    sums[...] = total
    block_list(tables.at[0], arranged, codes, slots, 0)
    block_list(tables.at[1], arranged, codes, slots, 1)
    for copy in copies[:2]:
        copy.wait()
    block_list(tables.at[2], arranged, codes, slots, 2)
    block_list(tables.at[3], arranged, codes, slots, 3)
    for copy in copies[2:]:
        copy.wait()


def pack_row(source, packed):
    value = source[...]
    half = value.shape[0] // 2
    peak = jnp.maximum(jnp.max(jnp.abs(value), axis=1, keepdims=True), 1e-30)
    level = jnp.round(value * (LEVELS / peak)).astype(jnp.int32)
    both = level[:half] * 65536 + level[half:]
    for block in range(packed.shape[0]):
        packed[block] = both[:, block * LANES : (block + 1) * LANES]
    return peak * (1.0 / LEVELS)


def unpack(total, step):
    half = total.shape[0]
    second = jnp.right_shift(jnp.left_shift(total, 16), 16)
    first = jnp.right_shift(total - second, 16)
    return first.astype(F32) * step[:half], second.astype(F32) * step[half:]


def linked_rows(jobs, tables, codes, slots, packed, links, between=()):
    blocks, half = packed.shape[1:3]

    def moved(values, lane):
        return lax.gather(
            values, lane[..., None], GATHER, (1, 1), mode=lax.GatherScatterMode.PROMISE_IN_BOUNDS
        )

    def put(which, out_lanes, total, step):
        first, second = unpack(total, step)
        links[which, 0:half, out_lanes] = first
        links[which, half : 2 * half, out_lanes] = second

    steps = {which: pack_row(source, packed.at[which]) for source, which in jobs}
    for block in range(blocks):
        out_lanes = slice(block * LANES, (block + 1) * LANES)
        for _, which in jobs:
            total = None
            for entry in range(3):
                first, second = slots[which, block, entry], slots[which, block, 3 + entry]
                code = jnp.broadcast_to(codes[which, entry, block : block + 1, :], (2 * half, LANES))
                values = jnp.concatenate([packed[which, first], packed[which, second]], axis=0)
                arrived = moved(values, jnp.bitwise_and(code, LANES - 1))
                code = code[:half]
                picked = jnp.where(code < LANES, arrived[:half], jnp.where(code < 2 * LANES, arrived[half:], 0))
                total = picked if total is None else total + picked
            put(which, out_lanes, total, steps[which])
        for work in between[block::blocks]:
            work()

    def general(which):
        @pl.when(slots[which, 0, 6] > 0)
        def _():
            @pl.loop(0, blocks)
            def _(block):
                out_lanes = pl.ds(pl.multiple_of(block * LANES, LANES), LANES)

                def add(origin, total):
                    values = packed[which, origin]
                    for entry in range(3):
                        index = jnp.broadcast_to(tables[which, entry, :, out_lanes], (half, LANES))
                        arrived = moved(values, jnp.bitwise_and(index, LANES - 1))
                        total = total + jnp.where(jnp.right_shift(index, 7) == origin, arrived, 0)
                    return total

                total = lax.fori_loop(0, blocks, add, jnp.zeros((half, LANES), jnp.int32))
                put(which, out_lanes, total, steps[which])

    @pl.when(functools.reduce(jnp.maximum, [slots[which, 0, 6] for _, which in jobs]) > 0)
    def _():
        for _, which in jobs:
            general(which)


def edge_kernel(fields, inner_split, slots, codes, tables, split, second, third, last_links, fresh, links, packed):
    rows = inner_split.shape[0]
    channels = fields.shape[2]
    orders = fields.shape[0] + 1
    top = HALO
    bottom = HALO + rows - 1
    mirror = 2 * HALO + rows - 1

    def field(order, row):
        if order == 0 or HALO + order <= row <= bottom - order:
            return fields.at[order, row]
        side, depth = (0, row - HALO) if row <= HALO + order else (1, bottom - row)
        if depth >= 0 and order == orders - 3:
            return second.at[side, depth]
        if depth >= 0 and order == orders - 2:
            return third.at[side, depth]
        return fresh.at[order - 1, side, depth + HALO - order]

    def edge(r):
        return r if r < HALO else r - rows + 2 * HALO

    def copy_terms(row, depth):
        known = slice(0, channels * TERMS.index((depth + 1, 0)))
        split[edge(row), known] = inner_split[row, known]

    def copy_field(target, order, side, depth):
        target[side, depth] = fields[order, top + depth if side == 0 else bottom - depth]

    copies = []
    for depth in range(HALO + 1):
        for side in range(2):
            row = depth if side == 0 else rows - 1 - depth
            if depth < HALO:
                copies.append(functools.partial(copy_terms, row, depth))
            if orders - 3 <= depth < HALO:
                copies.append(functools.partial(copy_field, second, orders - 3, side, depth))
            if depth >= orders - 2:
                copies.append(functools.partial(copy_field, third, orders - 2, side, depth))

    def sweep(order, row):
        last = order == orders - 1
        upper, lower, link = field(order - 1, row - 1), field(order - 1, row + 1), None
        if row == top:
            upper, link = None, links.at[0]
        elif row == bottom:
            lower, link = None, links.at[1]
        elif row == top - 1:
            lower, link = None, links.at[2]
        elif row == bottom + 1:
            upper, link = None, links.at[3]
        sweep_row(
            order, upper, field(order - 1, row), lower, field(order - 2, row) if order > 1 else None,
            link=link, field=None if last else field(order, row),
            split=split.at[edge(row - HALO)] if top <= row <= bottom else None,
        )

    for order in range(1, orders):
        last = order == orders - 1
        jobs = [(field(order - 1, top - 1), 0), (field(order - 1, bottom + 1), 1)]
        if not last:
            jobs += [(field(order - 1, top), 2), (field(order - 1, bottom), 3)]
        swept = [row for near in range(order, HALO + order) for row in (near, mirror - near)]
        linked = [row for row in swept if row in (top - 1, top, bottom, bottom + 1)]
        between = [functools.partial(sweep, order, row) for row in swept if row not in linked]
        if order == 1:
            between += copies
        linked_rows(jobs, tables, codes, slots, packed, last_links if last else links, between)
        if not last:
            for row in linked:
                sweep(order, row)


def sum_kernel(
    sky, inner,
    split, edge_split, second, third, last_links, acts, inner_sums, left,
    flat, total,
    newest, part_in, part_out, in_send, in_recv, out_send, out_recv,
):
    rows, stacked, columns = split.shape
    orders = HALO + 1
    channels = stacked // len(TERMS)
    outer = sky // inner
    me = lax.axis_index("sky")
    slot = lax.rem(me, inner)
    group = lax.div(me, inner)

    def in_peer(step):
        return group * inner + lax.rem(slot + step, inner)

    def out_peer(step):
        return lax.rem(group + step, outer) * inner + slot

    barrier = pltpu.get_barrier_semaphore()
    peers = [in_peer(step) for step in range(1, inner)] + [out_peer(step) for step in range(1, outer)]
    for peer in peers:
        pl.semaphore_signal(barrier, inc=1, device_id={"sky": peer}, device_id_type=MESH)

    for side in range(2):
        sweep_row(
            orders - 1, None, third.at[side, 0], third.at[side, 1], second.at[side, 0],
            link=last_links.at[side], split=newest.at[side], start=0,
        )

    def edge_rows():
        return [(r, r) for r in range(HALO)] + [(rows - 2 * HALO + r, r) for r in range(HALO, 2 * HALO)]

    known = stacked - newest.shape[1]
    outermost = {0: 0, rows - 1: 1}
    sums = inner_sums[...]
    for r, at in edge_rows():
        if r not in outermost:
            sums += lax.dot_general(acts[r], edge_split[at], CONTRACT_LAST, preferred_element_type=F32)
    old_sums = jnp.zeros((acts.shape[1], known), F32)
    new_sums = jnp.zeros((acts.shape[1], stacked - known), F32)
    for r, at in edge_rows():
        if r in outermost:
            old_sums += lax.dot_general(acts[r], edge_split[at, 0:known], CONTRACT_LAST, preferred_element_type=F32)
            new_sums += lax.dot_general(acts[r], newest[outermost[r]], CONTRACT_LAST, preferred_element_type=F32)
    sums += jnp.concatenate([old_sums, new_sums], axis=1)
    part_in[slot] = sums[0:channels] + sums[channels : 2 * channels]
    pl.semaphore_wait(barrier, len(peers))

    def exchange(buffer, own, count, peer_of, send, recv):
        copies = [
            remote(buffer.at[own], buffer.at[own], send.at[step], recv.at[step], peer_of(step))
            for step in range(1, count)
        ]
        for copy in copies:
            copy.start()
        return copies

    def total_of(buffer, copies):
        for copy in copies:
            copy.wait()
        return functools.reduce(lambda total, i: total + buffer[i], range(1, len(copies) + 1), buffer[0])

    copies = exchange(part_in, slot, inner, in_peer, in_send, in_recv)
    for r, at in edge_rows():
        if r in outermost:
            flat[:, r, :] = jnp.dot(left[:, :known], edge_split[at, 0:known], preferred_element_type=F32) + jnp.dot(
                left[:, known:], newest[outermost[r]], preferred_element_type=F32
            )
        else:
            flat[:, r, :] = jnp.dot(left[...], edge_split[at], preferred_element_type=F32)
    part_out[group] = total_of(part_in, copies)
    copies = exchange(part_out, group, outer, out_peer, out_send, out_recv)
    for r in range(HALO, rows - HALO):
        flat[:, r, :] = jnp.dot(left[...], split[r], preferred_element_type=F32)
    total[...] = total_of(part_out, copies)


def result_kernel(norm, flat, total, out, weight_grad):
    channels = out.shape[0]
    for channel in range(channels):
        out[channel] = flat[channel].astype(BF16)
    scaled = total[...] * norm
    for k in range(weight_grad.shape[0]):
        parts = [scaled[:, channels * i : channels * (i + 1)] for i, (order, _) in enumerate(TERMS) if order == k]
        weight_grad[k] = functools.reduce(jnp.add, parts)


def on_device(sky, saved_acts, scales, grad_out, weights, edge_up, edge_down):
    channels, rows, columns = saved_acts.shape
    orders = weights.shape[0]
    blocks = scales.shape[2]
    inner = min(8, sky)
    outer = sky // inner
    norm = 1.0 / math.sqrt(rows * columns * sky)
    stacked = channels * len(TERMS)
    known = channels * TERMS.index((orders - 1, 0))
    edge = 2 * HALO
    vmem = pl.BlockSpec(memory_space=pltpu.VMEM)
    smem = pl.BlockSpec(memory_space=pltpu.SMEM)
    hbm = pl.BlockSpec(memory_space=pltpu.HBM)
    dma = pltpu.SemaphoreType.DMA
    shape = jax.ShapeDtypeStruct
    up, down = jnp.transpose(edge_up, (1, 0, 2)), jnp.transpose(edge_down, (1, 0, 2))
    fields, split, acts, sums, slots, codes, tables, left = pl.pallas_call(
        functools.partial(exchange_kernel, sky),
        out_shape=(
            shape((orders - 1, rows + 2 * HALO, channels, columns), F32),
            shape((rows, stacked, columns), BF16),
            shape((rows, 2 * channels, columns), BF16),
            shape((2 * channels, stacked), F32),
            shape((4, columns // LANES, LANES), jnp.int32),
            shape((4, 3, columns // LANES, LANES), jnp.int32),
            shape((4, 3, 1, columns), jnp.int32),
            shape((channels, stacked), BF16),
        ),
        in_specs=[hbm] * 6,
        out_specs=(vmem,) * 8,
        scratch_shapes=[
            pltpu.VMEM((channels, rows, columns), BF16),
            pltpu.VMEM((channels, rows, blocks), F32),
            pltpu.VMEM((channels, rows, columns), BF16),
            pltpu.VMEM((orders, channels, channels), BF16),
            pltpu.VMEM((channels, rows, columns), F32),
            pltpu.VMEM((rows, channels, columns), F32),
            pltpu.VMEM((rows, channels, blocks), F32),
            pltpu.VMEM((3, columns // LANES, LANES), jnp.int32),
            dma((2, HALO)), dma((2, HALO)), dma((2,)), dma((2,)), dma((channels // 4 + 5,)),
        ],
        compiler_params=pltpu.CompilerParams(
            collective_id=0, has_side_effects=True, vmem_limit_bytes=12 * 2**20
        ),
        name="exchange",
    )(*(pltpu.with_memory_space_constraint(x, pltpu.HBM) for x in (saved_acts, scales, grad_out, weights, up, down)))
    edge_split, second, third, last_links = pl.pallas_call(
        edge_kernel,
        out_shape=(
            shape((edge, stacked, columns), BF16),
            shape((2, HALO, channels, columns), F32),
            shape((2, HALO + 1, channels, columns), F32),
            shape((2, channels, columns), F32),
        ),
        in_specs=[vmem, vmem, smem, vmem, vmem],
        out_specs=(vmem,) * 4,
        scratch_shapes=[
            pltpu.VMEM((orders - 2, 2, HALO + 1, channels, columns), F32),
            pltpu.VMEM((4, channels, columns), F32),
            pltpu.VMEM((4, columns // LANES, channels // 2, LANES), jnp.int32),
        ],
        compiler_params=pltpu.CompilerParams(vmem_limit_bytes=12 * 2**20),
        name="edges",
    )(fields, split, slots, codes, tables)
    flat, total = pl.pallas_call(
        functools.partial(sum_kernel, sky, inner),
        out_shape=(shape((channels, rows, columns), F32), shape((channels, stacked), F32)),
        in_specs=[vmem] * 8,
        out_specs=(vmem, vmem),
        scratch_shapes=[
            pltpu.VMEM((2, stacked - known, columns), BF16),
            pltpu.VMEM((inner, channels, stacked), F32),
            pltpu.VMEM((outer, channels, stacked), F32),
            dma((inner,)), dma((inner,)), dma((outer,)), dma((outer,)),
        ],
        compiler_params=pltpu.CompilerParams(
            collective_id=1, has_side_effects=True, vmem_limit_bytes=12 * 2**20
        ),
        name="sky_sum",
    )(split, edge_split, second, third, last_links, acts, sums, left)
    return pl.pallas_call(
        functools.partial(result_kernel, norm),
        out_shape=(shape((channels, rows, columns), BF16), shape((orders, channels, channels), F32)),
        in_specs=[vmem] * 2,
        out_specs=(vmem, vmem),
        compiler_params=pltpu.CompilerParams(vmem_limit_bytes=12 * 2**20),
        name="results",
    )(flat, total)


def solution(mesh):
    return jax.shard_map(
        functools.partial(on_device, mesh.shape["sky"]),
        mesh=mesh,
        in_specs=(
            P("rep", "sky", None),
            P("rep", "sky", None),
            P("rep", "sky", None),
            P(),
            P("sky", None, None),
            P("sky", None, None),
        ),
        out_specs=(P("rep", "sky", None), P("rep", None, None)),
        check_vma=False,
    )
```

```python
import functools
import math

import jax
import jax.numpy as jnp
from jax import lax
from jax.experimental import pallas as pl
from jax.experimental.pallas import tpu as pltpu
from jax.sharding import PartitionSpec as P

F32 = jnp.float32
BF16 = jnp.bfloat16
LANES = 128
HALO = 4
MESH = pl.DeviceIdType.MESH
CONTRACT_LAST = (((1,), (1,)), ((), ()))
TERMS = ((0, 0), (1, 0), (2, 0), (2, 1), (3, 0), (3, 1), (4, 0), (4, 1))
LEVELS = 10922.0
GATHER = lax.GatherDimensionNumbers(
    offset_dims=(), collapsed_slice_dims=(1,), start_index_map=(1,),
    operand_batching_dims=(0,), start_indices_batching_dims=(0,),
)


def split_bf16(value):
    high = value.astype(BF16)
    low = (value - high.astype(F32)).astype(BF16)
    return high, low


def remote(source, target, send, recv, peer):
    return pltpu.make_async_remote_copy(
        src_ref=source, dst_ref=target, send_sem=send, recv_sem=recv,
        device_id={"sky": peer}, device_id_type=MESH,
    )


def sweep_row(order, upper, middle, lower, older, link=None, field=None, split=None, start=None):
    channels, columns = middle.shape
    blocks = columns // LANES
    if start is None:
        start = channels * TERMS.index((order, 0))
    lane = lax.broadcasted_iota(jnp.int32, (channels, LANES), 1)
    sums = []
    for block in range(blocks):
        lanes = slice(block * LANES, (block + 1) * LANES)
        value = middle[:, lanes]
        if upper is not None:
            value = value + upper[:, lanes]
        if lower is not None:
            value = value + lower[:, lanes]
        sums.append(value)
    right_moved = [pltpu.roll(value, 1, 1) for value in sums]
    left_moved = [pltpu.roll(value, LANES - 1, 1) for value in sums]
    for block in range(blocks):
        lanes = slice(block * LANES, (block + 1) * LANES)
        from_left = jnp.where(lane == 0, right_moved[block - 1] if block > 0 else 0.0, right_moved[block])
        from_right = jnp.where(
            lane == LANES - 1, left_moved[block + 1] if block < blocks - 1 else 0.0, left_moved[block]
        )
        total = sums[block] + from_left + from_right - middle[:, lanes]
        if link is not None:
            total = total + link[:, lanes]
        if order == 1:
            result = -0.125 * total
        else:
            result = -0.25 * total - older[:, lanes]
        if field is not None:
            field[:, lanes] = result
        if split is not None:
            if order == 1:
                split[start : start + channels, lanes] = result.astype(BF16)
            else:
                high, low = split_bf16(result)
                split[start : start + channels, lanes] = high
                split[start + channels : start + 2 * channels, lanes] = low


def stacked_weights(weights):
    return jnp.concatenate([weights[k] for k, _ in TERMS], axis=1)


def block_list(table, arranged, codes, slots, which):
    blocks = table.shape[-1] // LANES
    for entry in range(3):
        for block in range(blocks):
            arranged[entry, block : block + 1, :] = table[entry, :, block * LANES : (block + 1) * LANES]
    lane = lax.broadcasted_iota(jnp.int32, (blocks, LANES), 1)
    packed = jnp.zeros((blocks, LANES), jnp.int32)
    more = jnp.zeros((blocks, 1), jnp.int32)
    for entry in range(3):
        index = arranged[entry]
        home = jnp.right_shift(index, 7)
        first = jnp.min(home, axis=1, keepdims=True)
        second = jnp.min(jnp.where(home > first, home, blocks), axis=1, keepdims=True)
        third = jnp.min(jnp.where(home > second, home, blocks), axis=1, keepdims=True)
        first = jnp.minimum(first, blocks - 1)
        second = jnp.minimum(second, blocks - 1)
        slot = jnp.where(home == first, 0, jnp.where(home == second, LANES, 2 * LANES))
        codes[which, entry] = jnp.bitwise_and(index, LANES - 1) + slot
        packed = jnp.where(lane == entry, first, packed)
        packed = jnp.where(lane == 3 + entry, second, packed)
        more = jnp.maximum(more, (third < blocks).astype(jnp.int32))
    slots[which] = jnp.where(lane == 6, jnp.max(more, axis=0, keepdims=True), packed)


def exchange_kernel(
    sky,
    saved_hbm, scales_hbm, grad_hbm, weights_hbm, up_hbm, down_hbm,
    fields, split, acts, sums, slots, codes, tables, left,
    saved, scales, grad, weights, flat, rows_x, scale_rows, arranged,
    halo_send, halo_recv, table_send, table_recv, load,
):
    channels, rows, columns = saved.shape
    orders = weights.shape[0]
    blocks = scales.shape[2]
    width = columns // blocks
    me = lax.axis_index("sky")
    before = lax.rem(me + sky - 1, sky)
    after = lax.rem(me + 1, sky)

    barrier = pltpu.get_barrier_semaphore()
    for peer in (before, after):
        pl.semaphore_signal(barrier, inc=1, device_id={"sky": peer}, device_id_type=MESH)
    loads = [
        pltpu.make_async_copy(source, target, load.at[i])
        for i, (source, target) in enumerate(
            [
                *((grad_hbm.at[pl.ds(4 * i, 4)], grad.at[pl.ds(4 * i, 4)]) for i in range(channels // 4)),
                (up_hbm, tables.at[0]),
                (down_hbm, tables.at[1]),
                (saved_hbm, saved),
                (scales_hbm, scales),
                (weights_hbm, weights),
            ]
        )
    ]
    for copy in loads:
        copy.start()

    chunks = channels // 4
    for channel in range(channels):
        if channel % 4 == 0:
            loads[channel // 4].wait()
        flat[channel] = grad[channel].astype(F32)
    edge_first = [r for i in range(HALO) for r in (rows - 1 - i, i)]
    for r in edge_first:
        fields[0, HALO + r] = flat[:, r, :]
    loads[chunks].wait()
    loads[chunks + 1].wait()
    pl.semaphore_wait(barrier, 2)

    copies = [
        remote(tables.at[0], tables.at[3], table_send.at[0], table_recv.at[0], before),
        remote(tables.at[1], tables.at[2], table_send.at[1], table_recv.at[1], after),
    ]
    for i in range(HALO):
        copies += [
            remote(fields.at[0, HALO + i], fields.at[0, HALO + rows + i], halo_send.at[0, i], halo_recv.at[0, i], before),
            remote(fields.at[0, HALO + rows - 1 - i], fields.at[0, HALO - 1 - i], halo_send.at[1, i], halo_recv.at[1, i], after),
        ]
    for copy in copies:
        copy.start()

    for r in range(HALO, rows - HALO):
        fields[0, HALO + r] = flat[:, r, :]

    @pl.loop(0, rows)
    def _(r):
        split[r, 0:channels] = fields[0, HALO + r].astype(BF16)

    for order in range(1, orders):
        @pl.loop(order, rows - order, step=2)
        def _(start):
            for r in (start, start + 1):
                row = HALO + r
                sweep_row(
                    order, fields.at[order - 1, row - 1], fields.at[order - 1, row], fields.at[order - 1, row + 1],
                    fields.at[order - 2, row] if order > 1 else None,
                    field=fields.at[order, row] if order < orders - 1 else None, split=split.at[r],
                )

    for copy in loads[chunks + 2 :]:
        copy.wait()
    for channel in range(channels):
        flat[channel] = saved[channel].astype(F32)
    for r in range(rows):
        rows_x[r] = flat[:, r, :]
        scale_rows[r] = scales[:, r, :]

    @pl.loop(0, rows)
    def _(r):
        for block in range(blocks):
            lanes = slice(block * width, (block + 1) * width)
            high, low = split_bf16(rows_x[r, :, lanes] * scale_rows[r, :, block : block + 1])
            acts[r, 0:channels, lanes] = high
            acts[r, channels : 2 * channels, lanes] = low

    left[...] = stacked_weights(weights)
    total = jnp.zeros(sums.shape, F32)
    for r in range(HALO, rows - HALO):
        total += lax.dot_general(acts[r], split[r], CONTRACT_LAST, preferred_element_type=F32)
    sums[...] = total
    block_list(tables.at[0], arranged, codes, slots, 0)
    block_list(tables.at[1], arranged, codes, slots, 1)
    for copy in copies[:2]:
        copy.wait()
    block_list(tables.at[2], arranged, codes, slots, 2)
    block_list(tables.at[3], arranged, codes, slots, 3)
    for copy in copies[2:]:
        copy.wait()


def pack_row(source, packed):
    value = source[...]
    half = value.shape[0] // 2
    peak = jnp.maximum(jnp.max(jnp.abs(value), axis=1, keepdims=True), 1e-30)
    level = jnp.round(value * (LEVELS / peak)).astype(jnp.int32)
    both = level[:half] * 65536 + level[half:]
    for block in range(packed.shape[0]):
        packed[block] = both[:, block * LANES : (block + 1) * LANES]
    return peak * (1.0 / LEVELS)


def unpack(total, step):
    half = total.shape[0]
    second = jnp.right_shift(jnp.left_shift(total, 16), 16)
    first = jnp.right_shift(total - second, 16)
    return first.astype(F32) * step[:half], second.astype(F32) * step[half:]


def linked_rows(jobs, tables, codes, slots, packed, links, between=()):
    blocks, half = packed.shape[1:3]

    def moved(values, lane):
        return lax.gather(
            values, lane[..., None], GATHER, (1, 1), mode=lax.GatherScatterMode.PROMISE_IN_BOUNDS
        )

    def put(which, out_lanes, total, step):
        first, second = unpack(total, step)
        links[which, 0:half, out_lanes] = first
        links[which, half : 2 * half, out_lanes] = second

    steps = {which: pack_row(source, packed.at[which]) for source, which in jobs}
    for block in range(blocks):
        out_lanes = slice(block * LANES, (block + 1) * LANES)
        for _, which in jobs:
            total = None
            for entry in range(3):
                first, second = slots[which, block, entry], slots[which, block, 3 + entry]
                code = jnp.broadcast_to(codes[which, entry, block : block + 1, :], (half, LANES))
                lane = jnp.bitwise_and(code, LANES - 1)
                values = jnp.concatenate([packed[which, first], packed[which, second]], axis=0)
                arrived = moved(values, jnp.concatenate([lane, lane], axis=0))
                picked = jnp.where(code < LANES, arrived[:half], jnp.where(code < 2 * LANES, arrived[half:], 0))
                total = picked if total is None else total + picked
            put(which, out_lanes, total, steps[which])
        for work in between[block::blocks]:
            work()

    def general(which):
        @pl.when(slots[which, 0, 6] > 0)
        def _():
            @pl.loop(0, blocks)
            def _(block):
                out_lanes = pl.ds(pl.multiple_of(block * LANES, LANES), LANES)

                def add(origin, total):
                    values = packed[which, origin]
                    for entry in range(3):
                        index = jnp.broadcast_to(tables[which, entry, :, out_lanes], (half, LANES))
                        arrived = moved(values, jnp.bitwise_and(index, LANES - 1))
                        total = total + jnp.where(jnp.right_shift(index, 7) == origin, arrived, 0)
                    return total

                total = lax.fori_loop(0, blocks, add, jnp.zeros((half, LANES), jnp.int32))
                put(which, out_lanes, total, steps[which])

    @pl.when(functools.reduce(jnp.maximum, [slots[which, 0, 6] for _, which in jobs]) > 0)
    def _():
        for _, which in jobs:
            general(which)


def edge_kernel(fields, inner_split, slots, codes, tables, split, second, third, last_links, fresh, links, packed):
    rows = inner_split.shape[0]
    channels = fields.shape[2]
    orders = fields.shape[0] + 1
    top = HALO
    bottom = HALO + rows - 1
    mirror = 2 * HALO + rows - 1

    def field(order, row):
        if order == 0 or HALO + order <= row <= bottom - order:
            return fields.at[order, row]
        side, depth = (0, row - HALO) if row <= HALO + order else (1, bottom - row)
        if depth >= 0 and order == orders - 3:
            return second.at[side, depth]
        if depth >= 0 and order == orders - 2:
            return third.at[side, depth]
        return fresh.at[order - 1, side, depth + HALO - order]

    def edge(r):
        return r if r < HALO else r - rows + 2 * HALO

    def copy_terms(row, depth):
        known = slice(0, channels * TERMS.index((depth + 1, 0)))
        split[edge(row), known] = inner_split[row, known]

    def copy_field(target, order, side, depth):
        target[side, depth] = fields[order, top + depth if side == 0 else bottom - depth]

    copies = []
    for depth in range(HALO + 1):
        for side in range(2):
            row = depth if side == 0 else rows - 1 - depth
            if depth < HALO:
                copies.append(functools.partial(copy_terms, row, depth))
            if orders - 3 <= depth < HALO:
                copies.append(functools.partial(copy_field, second, orders - 3, side, depth))
            if depth >= orders - 2:
                copies.append(functools.partial(copy_field, third, orders - 2, side, depth))

    def sweep(order, row):
        last = order == orders - 1
        upper, lower, link = field(order - 1, row - 1), field(order - 1, row + 1), None
        if row == top:
            upper, link = None, links.at[0]
        elif row == bottom:
            lower, link = None, links.at[1]
        elif row == top - 1:
            lower, link = None, links.at[2]
        elif row == bottom + 1:
            upper, link = None, links.at[3]
        sweep_row(
            order, upper, field(order - 1, row), lower, field(order - 2, row) if order > 1 else None,
            link=link, field=None if last else field(order, row),
            split=split.at[edge(row - HALO)] if top <= row <= bottom else None,
        )

    for order in range(1, orders):
        last = order == orders - 1
        jobs = [(field(order - 1, top - 1), 0), (field(order - 1, bottom + 1), 1)]
        if not last:
            jobs += [(field(order - 1, top), 2), (field(order - 1, bottom), 3)]
        swept = [row for near in range(order, HALO + order) for row in (near, mirror - near)]
        linked = [row for row in swept if row in (top - 1, top, bottom, bottom + 1)]
        between = [functools.partial(sweep, order, row) for row in swept if row not in linked]
        if order == 1:
            between += copies
        linked_rows(jobs, tables, codes, slots, packed, last_links if last else links, between)
        if not last:
            for row in linked:
                sweep(order, row)


def farthest_first(count):
    return sorted(range(1, count), key=lambda step: -min(step, count - step))


def sum_kernel(
    sky, inner,
    split, edge_split, second, third, last_links, acts, inner_sums, left,
    rounded, total,
    flat, newest, part_in, part_out, in_send, in_recv, out_send, out_recv,
):
    rows, stacked, columns = split.shape
    orders = HALO + 1
    channels = stacked // len(TERMS)
    outer = sky // inner
    me = lax.axis_index("sky")
    slot = lax.rem(me, inner)
    group = lax.div(me, inner)

    def in_peer(step):
        return group * inner + lax.rem(slot + step, inner)

    def out_peer(step):
        return lax.rem(group + step, outer) * inner + slot

    barrier = pltpu.get_barrier_semaphore()
    peers = [out_peer(step) for step in farthest_first(outer)] + [in_peer(step) for step in farthest_first(inner)]
    for peer in peers:
        pl.semaphore_signal(barrier, inc=1, device_id={"sky": peer}, device_id_type=MESH)

    for side in range(2):
        sweep_row(
            orders - 1, None, third.at[side, 0], third.at[side, 1], second.at[side, 0],
            link=last_links.at[side], split=newest.at[side], start=0,
        )

    def edge_rows():
        return [(r, r) for r in range(HALO)] + [(rows - 2 * HALO + r, r) for r in range(HALO, 2 * HALO)]

    known = stacked - newest.shape[1]
    outermost = {0: 0, rows - 1: 1}
    sums = inner_sums[...]
    for r, at in edge_rows():
        if r not in outermost:
            sums += lax.dot_general(acts[r], edge_split[at], CONTRACT_LAST, preferred_element_type=F32)
    old_sums = jnp.zeros((acts.shape[1], known), F32)
    new_sums = jnp.zeros((acts.shape[1], stacked - known), F32)
    for r, at in edge_rows():
        if r in outermost:
            old_sums += lax.dot_general(acts[r], edge_split[at, 0:known], CONTRACT_LAST, preferred_element_type=F32)
            new_sums += lax.dot_general(acts[r], newest[outermost[r]], CONTRACT_LAST, preferred_element_type=F32)
    sums += jnp.concatenate([old_sums, new_sums], axis=1)
    part_in[slot] = sums[0:channels] + sums[channels : 2 * channels]
    pl.semaphore_wait(barrier, len(peers))

    def exchange(buffer, own, count, peer_of, send, recv):
        copies = [
            remote(buffer.at[own], buffer.at[own], send.at[step], recv.at[step], peer_of(step))
            for step in farthest_first(count)
        ]
        for copy in copies:
            copy.start()
        return copies

    def total_of(buffer, copies):
        for copy in copies:
            copy.wait()
        return functools.reduce(lambda total, i: total + buffer[i], range(1, len(copies) + 1), buffer[0])

    copies = exchange(part_in, slot, inner, in_peer, in_send, in_recv)
    for r, at in edge_rows():
        if r in outermost:
            flat[:, r, :] = jnp.dot(left[:, :known], edge_split[at, 0:known], preferred_element_type=F32) + jnp.dot(
                left[:, known:], newest[outermost[r]], preferred_element_type=F32
            )
        else:
            flat[:, r, :] = jnp.dot(left[...], edge_split[at], preferred_element_type=F32)
    part_out[group] = total_of(part_in, copies)
    copies = exchange(part_out, group, outer, out_peer, out_send, out_recv)
    for r in range(HALO, rows - HALO):
        flat[:, r, :] = jnp.dot(left[...], split[r], preferred_element_type=F32)
    for channel in range(channels):
        rounded[channel] = flat[channel].astype(BF16)
    total[...] = total_of(part_out, copies)


def result_kernel(norm, rounded, total, out, weight_grad):
    channels = out.shape[0]
    out[...] = rounded[...]
    scaled = total[...] * norm
    for k in range(weight_grad.shape[0]):
        parts = [scaled[:, channels * i : channels * (i + 1)] for i, (order, _) in enumerate(TERMS) if order == k]
        weight_grad[k] = functools.reduce(jnp.add, parts)


def on_device(sky, saved_acts, scales, grad_out, weights, edge_up, edge_down):
    channels, rows, columns = saved_acts.shape
    orders = weights.shape[0]
    blocks = scales.shape[2]
    inner = min(8, sky)
    outer = sky // inner
    norm = 1.0 / math.sqrt(rows * columns * sky)
    stacked = channels * len(TERMS)
    known = channels * TERMS.index((orders - 1, 0))
    edge = 2 * HALO
    vmem = pl.BlockSpec(memory_space=pltpu.VMEM)
    smem = pl.BlockSpec(memory_space=pltpu.SMEM)
    hbm = pl.BlockSpec(memory_space=pltpu.HBM)
    dma = pltpu.SemaphoreType.DMA
    shape = jax.ShapeDtypeStruct
    up, down = jnp.transpose(edge_up, (1, 0, 2)), jnp.transpose(edge_down, (1, 0, 2))
    fields, split, acts, sums, slots, codes, tables, left = pl.pallas_call(
        functools.partial(exchange_kernel, sky),
        out_shape=(
            shape((orders - 1, rows + 2 * HALO, channels, columns), F32),
            shape((rows, stacked, columns), BF16),
            shape((rows, 2 * channels, columns), BF16),
            shape((2 * channels, stacked), F32),
            shape((4, columns // LANES, LANES), jnp.int32),
            shape((4, 3, columns // LANES, LANES), jnp.int32),
            shape((4, 3, 1, columns), jnp.int32),
            shape((channels, stacked), BF16),
        ),
        in_specs=[hbm] * 6,
        out_specs=(vmem,) * 8,
        scratch_shapes=[
            pltpu.VMEM((channels, rows, columns), BF16),
            pltpu.VMEM((channels, rows, blocks), F32),
            pltpu.VMEM((channels, rows, columns), BF16),
            pltpu.VMEM((orders, channels, channels), BF16),
            pltpu.VMEM((channels, rows, columns), F32),
            pltpu.VMEM((rows, channels, columns), F32),
            pltpu.VMEM((rows, channels, blocks), F32),
            pltpu.VMEM((3, columns // LANES, LANES), jnp.int32),
            dma((2, HALO)), dma((2, HALO)), dma((2,)), dma((2,)), dma((channels // 4 + 5,)),
        ],
        compiler_params=pltpu.CompilerParams(
            collective_id=0, has_side_effects=True, vmem_limit_bytes=12 * 2**20
        ),
        name="exchange",
    )(*(pltpu.with_memory_space_constraint(x, pltpu.HBM) for x in (saved_acts, scales, grad_out, weights, up, down)))
    edge_split, second, third, last_links = pl.pallas_call(
        edge_kernel,
        out_shape=(
            shape((edge, stacked, columns), BF16),
            shape((2, HALO, channels, columns), F32),
            shape((2, HALO + 1, channels, columns), F32),
            shape((2, channels, columns), F32),
        ),
        in_specs=[vmem, vmem, smem, vmem, vmem],
        out_specs=(vmem,) * 4,
        scratch_shapes=[
            pltpu.VMEM((orders - 2, 2, HALO + 1, channels, columns), F32),
            pltpu.VMEM((4, channels, columns), F32),
            pltpu.VMEM((4, columns // LANES, channels // 2, LANES), jnp.int32),
        ],
        compiler_params=pltpu.CompilerParams(vmem_limit_bytes=12 * 2**20),
        name="edges",
    )(fields, split, slots, codes, tables)
    rounded, total = pl.pallas_call(
        functools.partial(sum_kernel, sky, inner),
        out_shape=(shape((channels, rows, columns), BF16), shape((channels, stacked), F32)),
        in_specs=[vmem] * 8,
        out_specs=(vmem, vmem),
        scratch_shapes=[
            pltpu.VMEM((channels, rows, columns), F32),
            pltpu.VMEM((2, stacked - known, columns), BF16),
            pltpu.VMEM((inner, channels, stacked), F32),
            pltpu.VMEM((outer, channels, stacked), F32),
            dma((inner,)), dma((inner,)), dma((outer,)), dma((outer,)),
        ],
        compiler_params=pltpu.CompilerParams(
            collective_id=1, has_side_effects=True, vmem_limit_bytes=12 * 2**20
        ),
        name="sky_sum",
    )(split, edge_split, second, third, last_links, acts, sums, left)
    return pl.pallas_call(
        functools.partial(result_kernel, norm),
        out_shape=(shape((channels, rows, columns), BF16), shape((orders, channels, channels), F32)),
        in_specs=[vmem] * 2,
        out_specs=(vmem, vmem),
        compiler_params=pltpu.CompilerParams(vmem_limit_bytes=12 * 2**20),
        name="results",
    )(rounded, total)


def solution(mesh):
    return jax.shard_map(
        functools.partial(on_device, mesh.shape["sky"]),
        mesh=mesh,
        in_specs=(
            P("rep", "sky", None),
            P("rep", "sky", None),
            P("rep", "sky", None),
            P(),
            P("sky", None, None),
            P("sky", None, None),
        ),
        out_specs=(P("rep", "sky", None), P("rep", None, None)),
        check_vma=False,
    )
```

```python
import functools
import math

import jax
import jax.numpy as jnp
from jax import lax
from jax.experimental import pallas as pl
from jax.experimental.pallas import tpu as pltpu
from jax.sharding import PartitionSpec as P

F32 = jnp.float32
BF16 = jnp.bfloat16
LANES = 128
HALO = 4
MESH = pl.DeviceIdType.MESH
CONTRACT_LAST = (((1,), (1,)), ((), ()))
TERMS = ((0, 0), (1, 0), (2, 0), (2, 1), (3, 0), (3, 1), (4, 0), (4, 1))
LEVELS = 10922.0
GATHER = lax.GatherDimensionNumbers(
    offset_dims=(), collapsed_slice_dims=(1,), start_index_map=(1,),
    operand_batching_dims=(0,), start_indices_batching_dims=(0,),
)


def split_bf16(value):
    high = value.astype(BF16)
    low = (value - high.astype(F32)).astype(BF16)
    return high, low


def remote(source, target, send, recv, peer):
    return pltpu.make_async_remote_copy(
        src_ref=source, dst_ref=target, send_sem=send, recv_sem=recv,
        device_id={"sky": peer}, device_id_type=MESH,
    )


def sweep_row(order, upper, middle, lower, older, link=None, field=None, split=None, start=None):
    channels, columns = middle.shape
    blocks = columns // LANES
    if start is None:
        start = channels * TERMS.index((order, 0))
    lane = lax.broadcasted_iota(jnp.int32, (channels, LANES), 1)
    sums = []
    for block in range(blocks):
        lanes = slice(block * LANES, (block + 1) * LANES)
        value = middle[:, lanes]
        if upper is not None:
            value = value + upper[:, lanes]
        if lower is not None:
            value = value + lower[:, lanes]
        sums.append(value)
    right_moved = [pltpu.roll(value, 1, 1) for value in sums]
    left_moved = [pltpu.roll(value, LANES - 1, 1) for value in sums]
    for block in range(blocks):
        lanes = slice(block * LANES, (block + 1) * LANES)
        from_left = jnp.where(lane == 0, right_moved[block - 1] if block > 0 else 0.0, right_moved[block])
        from_right = jnp.where(
            lane == LANES - 1, left_moved[block + 1] if block < blocks - 1 else 0.0, left_moved[block]
        )
        total = sums[block] + from_left + from_right - middle[:, lanes]
        if link is not None:
            total = total + link[:, lanes]
        if order == 1:
            result = -0.125 * total
        else:
            result = -0.25 * total - older[:, lanes]
        if field is not None:
            field[:, lanes] = result
        if split is not None:
            if order == 1:
                split[start : start + channels, lanes] = result.astype(BF16)
            else:
                high, low = split_bf16(result)
                split[start : start + channels, lanes] = high
                split[start + channels : start + 2 * channels, lanes] = low


def stacked_weights(weights):
    return jnp.concatenate([weights[k] for k, _ in TERMS], axis=1)


def block_list(table, arranged, codes, slots, which):
    blocks = table.shape[-1] // LANES
    for entry in range(3):
        for block in range(blocks):
            arranged[entry, block : block + 1, :] = table[entry, :, block * LANES : (block + 1) * LANES]
    lane = lax.broadcasted_iota(jnp.int32, (blocks, LANES), 1)
    packed = jnp.zeros((blocks, LANES), jnp.int32)
    more = jnp.zeros((blocks, 1), jnp.int32)
    for entry in range(3):
        index = arranged[entry]
        home = jnp.right_shift(index, 7)
        first = jnp.min(home, axis=1, keepdims=True)
        second = jnp.min(jnp.where(home > first, home, blocks), axis=1, keepdims=True)
        third = jnp.min(jnp.where(home > second, home, blocks), axis=1, keepdims=True)
        first = jnp.minimum(first, blocks - 1)
        second = jnp.minimum(second, blocks - 1)
        slot = jnp.where(home == first, 0, jnp.where(home == second, LANES, 2 * LANES))
        codes[which, entry] = jnp.bitwise_and(index, LANES - 1) + slot
        packed = jnp.where(lane == entry, first, packed)
        packed = jnp.where(lane == 3 + entry, second, packed)
        more = jnp.maximum(more, (third < blocks).astype(jnp.int32))
    slots[which] = jnp.where(lane == 6, jnp.max(more, axis=0, keepdims=True), packed)


def exchange_kernel(
    sky,
    saved_hbm, scales_hbm, grad_hbm, weights_hbm, up_hbm, down_hbm,
    fields, split, acts, sums, slots, codes, tables, left,
    saved, scales, grad, weights, flat, rows_x, scale_rows, arranged,
    halo_send, halo_recv, table_send, table_recv, load,
):
    channels, rows, columns = saved.shape
    orders = weights.shape[0]
    blocks = scales.shape[2]
    width = columns // blocks
    me = lax.axis_index("sky")
    before = lax.rem(me + sky - 1, sky)
    after = lax.rem(me + 1, sky)

    barrier = pltpu.get_barrier_semaphore()
    for peer in (before, after):
        pl.semaphore_signal(barrier, inc=1, device_id={"sky": peer}, device_id_type=MESH)
    loads = [
        pltpu.make_async_copy(source, target, load.at[i])
        for i, (source, target) in enumerate(
            [
                *((grad_hbm.at[pl.ds(4 * i, 4)], grad.at[pl.ds(4 * i, 4)]) for i in range(channels // 4)),
                (up_hbm, tables.at[0]),
                (down_hbm, tables.at[1]),
                (saved_hbm, saved),
                (scales_hbm, scales),
                (weights_hbm, weights),
            ]
        )
    ]
    for copy in loads:
        copy.start()

    chunks = channels // 4
    for channel in range(channels):
        if channel % 4 == 0:
            loads[channel // 4].wait()
        flat[channel] = grad[channel].astype(F32)
    edge_first = [r for i in range(HALO) for r in (rows - 1 - i, i)]
    for r in edge_first:
        fields[0, HALO + r] = flat[:, r, :]
    loads[chunks].wait()
    loads[chunks + 1].wait()
    pl.semaphore_wait(barrier, 2)

    copies = [
        remote(tables.at[0], tables.at[3], table_send.at[0], table_recv.at[0], before),
        remote(tables.at[1], tables.at[2], table_send.at[1], table_recv.at[1], after),
    ]
    for i in range(HALO):
        copies += [
            remote(fields.at[0, HALO + i], fields.at[0, HALO + rows + i], halo_send.at[0, i], halo_recv.at[0, i], before),
            remote(fields.at[0, HALO + rows - 1 - i], fields.at[0, HALO - 1 - i], halo_send.at[1, i], halo_recv.at[1, i], after),
        ]
    for copy in copies:
        copy.start()

    for r in range(HALO, rows - HALO):
        fields[0, HALO + r] = flat[:, r, :]

    @pl.loop(0, rows)
    def _(r):
        split[r, 0:channels] = fields[0, HALO + r].astype(BF16)

    for order in range(1, orders):
        @pl.loop(order, rows - order, step=2)
        def _(start):
            for r in (start, start + 1):
                row = HALO + r
                sweep_row(
                    order, fields.at[order - 1, row - 1], fields.at[order - 1, row], fields.at[order - 1, row + 1],
                    fields.at[order - 2, row] if order > 1 else None,
                    field=fields.at[order, row] if order < orders - 1 else None, split=split.at[r],
                )

    for copy in loads[chunks + 2 :]:
        copy.wait()
    for channel in range(channels):
        flat[channel] = saved[channel].astype(F32)
    for r in range(rows):
        rows_x[r] = flat[:, r, :]
        scale_rows[r] = scales[:, r, :]

    @pl.loop(0, rows)
    def _(r):
        for block in range(blocks):
            lanes = slice(block * width, (block + 1) * width)
            high, low = split_bf16(rows_x[r, :, lanes] * scale_rows[r, :, block : block + 1])
            acts[r, 0:channels, lanes] = high
            acts[r, channels : 2 * channels, lanes] = low

    left[...] = stacked_weights(weights)
    total = jnp.zeros(sums.shape, F32)
    for r in range(HALO, rows - HALO):
        total += lax.dot_general(acts[r], split[r], CONTRACT_LAST, preferred_element_type=F32)
    sums[...] = total
    block_list(tables.at[0], arranged, codes, slots, 0)
    block_list(tables.at[1], arranged, codes, slots, 1)
    for copy in copies[:2]:
        copy.wait()
    block_list(tables.at[2], arranged, codes, slots, 2)
    block_list(tables.at[3], arranged, codes, slots, 3)
    for copy in copies[2:]:
        copy.wait()


def pack_row(source, packed):
    value = source[...]
    half = value.shape[0] // 2
    peak = jnp.maximum(jnp.max(jnp.abs(value), axis=1, keepdims=True), 1e-30)
    level = jnp.round(value * (LEVELS / peak)).astype(jnp.int32)
    both = level[:half] * 65536 + level[half:]
    for block in range(packed.shape[0]):
        packed[block] = both[:, block * LANES : (block + 1) * LANES]
    return peak * (1.0 / LEVELS)


def unpack(total, step):
    half = total.shape[0]
    second = jnp.right_shift(jnp.left_shift(total, 16), 16)
    first = jnp.right_shift(total - second, 16)
    return first.astype(F32) * step[:half], second.astype(F32) * step[half:]


def linked_rows(jobs, tables, codes, slots, packed, links, between=()):
    blocks, half = packed.shape[1:3]

    def moved(values, lane):
        return lax.gather(
            values, lane[..., None], GATHER, (1, 1), mode=lax.GatherScatterMode.PROMISE_IN_BOUNDS
        )

    def put(which, out_lanes, total, step):
        first, second = unpack(total, step)
        links[which, 0:half, out_lanes] = first
        links[which, half : 2 * half, out_lanes] = second

    steps = {which: pack_row(source, packed.at[which]) for source, which in jobs}
    for block in range(blocks):
        out_lanes = slice(block * LANES, (block + 1) * LANES)
        for _, which in jobs:
            total = None
            for entry in range(3):
                first, second = slots[which, block, entry], slots[which, block, 3 + entry]
                code = jnp.broadcast_to(codes[which, entry, block : block + 1, :], (half, LANES))
                lane = jnp.bitwise_and(code, LANES - 1)
                values = jnp.concatenate([packed[which, first], packed[which, second]], axis=0)
                arrived = moved(values, jnp.concatenate([lane, lane], axis=0))
                picked = jnp.where(code < LANES, arrived[:half], jnp.where(code < 2 * LANES, arrived[half:], 0))
                total = picked if total is None else total + picked
            put(which, out_lanes, total, steps[which])
        for work in between[block::blocks]:
            work()

    def general(which):
        @pl.when(slots[which, 0, 6] > 0)
        def _():
            @pl.loop(0, blocks)
            def _(block):
                out_lanes = pl.ds(pl.multiple_of(block * LANES, LANES), LANES)

                def add(origin, total):
                    values = packed[which, origin]
                    for entry in range(3):
                        index = jnp.broadcast_to(tables[which, entry, :, out_lanes], (half, LANES))
                        arrived = moved(values, jnp.bitwise_and(index, LANES - 1))
                        total = total + jnp.where(jnp.right_shift(index, 7) == origin, arrived, 0)
                    return total

                total = lax.fori_loop(0, blocks, add, jnp.zeros((half, LANES), jnp.int32))
                put(which, out_lanes, total, steps[which])

    @pl.when(functools.reduce(jnp.maximum, [slots[which, 0, 6] for _, which in jobs]) > 0)
    def _():
        for _, which in jobs:
            general(which)


def edge_kernel(fields, inner_split, slots, codes, tables, split, second, third, last_links, fresh, links, packed):
    rows = inner_split.shape[0]
    channels = fields.shape[2]
    orders = fields.shape[0] + 1
    top = HALO
    bottom = HALO + rows - 1
    mirror = 2 * HALO + rows - 1

    def field(order, row):
        if order == 0 or HALO + order <= row <= bottom - order:
            return fields.at[order, row]
        side, depth = (0, row - HALO) if row <= HALO + order else (1, bottom - row)
        if depth >= 0 and order == orders - 3:
            return second.at[side, depth]
        if depth >= 0 and order == orders - 2:
            return third.at[side, depth]
        return fresh.at[order - 1, side, depth + HALO - order]

    def edge(r):
        return r if r < HALO else r - rows + 2 * HALO

    def copy_terms(row, depth):
        known = slice(0, channels * TERMS.index((depth + 1, 0)))
        split[edge(row), known] = inner_split[row, known]

    def copy_field(target, order, side, depth):
        target[side, depth] = fields[order, top + depth if side == 0 else bottom - depth]

    copies = []
    for depth in range(HALO + 1):
        for side in range(2):
            row = depth if side == 0 else rows - 1 - depth
            if depth < HALO:
                copies.append(functools.partial(copy_terms, row, depth))
            if orders - 3 <= depth < HALO:
                copies.append(functools.partial(copy_field, second, orders - 3, side, depth))
            if depth >= orders - 2:
                copies.append(functools.partial(copy_field, third, orders - 2, side, depth))

    def sweep(order, row):
        last = order == orders - 1
        upper, lower, link = field(order - 1, row - 1), field(order - 1, row + 1), None
        if row == top:
            upper, link = None, links.at[0]
        elif row == bottom:
            lower, link = None, links.at[1]
        elif row == top - 1:
            lower, link = None, links.at[2]
        elif row == bottom + 1:
            upper, link = None, links.at[3]
        sweep_row(
            order, upper, field(order - 1, row), lower, field(order - 2, row) if order > 1 else None,
            link=link, field=None if last else field(order, row),
            split=split.at[edge(row - HALO)] if top <= row <= bottom else None,
        )

    for order in range(1, orders):
        last = order == orders - 1
        jobs = [(field(order - 1, top - 1), 0), (field(order - 1, bottom + 1), 1)]
        if not last:
            jobs += [(field(order - 1, top), 2), (field(order - 1, bottom), 3)]
        swept = [row for near in range(order, HALO + order) for row in (near, mirror - near)]
        linked = [row for row in swept if row in (top - 1, top, bottom, bottom + 1)]
        between = [functools.partial(sweep, order, row) for row in swept if row not in linked]
        if order == 1:
            between += copies
        linked_rows(jobs, tables, codes, slots, packed, last_links if last else links, between)
        if not last:
            for row in linked:
                sweep(order, row)


def farthest_first(count):
    return sorted(range(1, count), key=lambda step: -min(step, count - step))


def sum_kernel(
    sky, inner,
    split, edge_split, second, third, last_links, acts, inner_sums, left,
    rounded, total,
    flat, newest, part_in, part_out, in_send, in_recv, out_send, out_recv,
):
    rows, stacked, columns = split.shape
    orders = HALO + 1
    channels = stacked // len(TERMS)
    outer = sky // inner
    me = lax.axis_index("sky")
    slot = lax.rem(me, inner)
    group = lax.div(me, inner)

    def in_peer(step):
        return group * inner + lax.rem(slot + step, inner)

    def out_peer(step):
        return lax.rem(group + step, outer) * inner + slot

    barrier = pltpu.get_barrier_semaphore()
    peers = [out_peer(step) for step in farthest_first(outer)] + [in_peer(step) for step in farthest_first(inner)]
    for peer in peers:
        pl.semaphore_signal(barrier, inc=1, device_id={"sky": peer}, device_id_type=MESH)

    def edge_rows():
        return [(r, r) for r in range(HALO)] + [(rows - 2 * HALO + r, r) for r in range(HALO, 2 * HALO)]

    known = stacked - newest.shape[1]
    outermost = {0: 0, rows - 1: 1}
    sums = inner_sums[...]
    for r, at in edge_rows():
        if r not in outermost:
            sums += lax.dot_general(acts[r], edge_split[at], CONTRACT_LAST, preferred_element_type=F32)
    old_sums = jnp.zeros((acts.shape[1], known), F32)
    new_sums = jnp.zeros((acts.shape[1], stacked - known), F32)
    for r, at in edge_rows():
        if r in outermost:
            old_sums += lax.dot_general(acts[r], edge_split[at, 0:known], CONTRACT_LAST, preferred_element_type=F32)
    for side in range(2):
        sweep_row(
            orders - 1, None, third.at[side, 0], third.at[side, 1], second.at[side, 0],
            link=last_links.at[side], split=newest.at[side], start=0,
        )
    for r, at in edge_rows():
        if r in outermost:
            new_sums += lax.dot_general(acts[r], newest[outermost[r]], CONTRACT_LAST, preferred_element_type=F32)
    sums += jnp.concatenate([old_sums, new_sums], axis=1)
    part_in[slot] = sums[0:channels] + sums[channels : 2 * channels]
    pl.semaphore_wait(barrier, len(peers))

    def exchange(buffer, own, count, peer_of, send, recv):
        copies = [
            remote(buffer.at[own], buffer.at[own], send.at[step], recv.at[step], peer_of(step))
            for step in farthest_first(count)
        ]
        for copy in copies:
            copy.start()
        return copies

    def total_of(buffer, copies):
        for copy in copies:
            copy.wait()
        return functools.reduce(lambda total, i: total + buffer[i], range(1, len(copies) + 1), buffer[0])

    copies = exchange(part_in, slot, inner, in_peer, in_send, in_recv)
    for r, at in edge_rows():
        if r in outermost:
            flat[:, r, :] = jnp.dot(left[:, :known], edge_split[at, 0:known], preferred_element_type=F32) + jnp.dot(
                left[:, known:], newest[outermost[r]], preferred_element_type=F32
            )
        else:
            flat[:, r, :] = jnp.dot(left[...], edge_split[at], preferred_element_type=F32)
    part_out[group] = total_of(part_in, copies)
    copies = exchange(part_out, group, outer, out_peer, out_send, out_recv)
    for r in range(HALO, rows - HALO):
        flat[:, r, :] = jnp.dot(left[...], split[r], preferred_element_type=F32)
    for channel in range(channels):
        rounded[channel] = flat[channel].astype(BF16)
    total[...] = total_of(part_out, copies)


def result_kernel(norm, rounded, total, out, weight_grad):
    channels = out.shape[0]
    out[...] = rounded[...]
    scaled = total[...] * norm
    for k in range(weight_grad.shape[0]):
        parts = [scaled[:, channels * i : channels * (i + 1)] for i, (order, _) in enumerate(TERMS) if order == k]
        weight_grad[k] = functools.reduce(jnp.add, parts)


def on_device(sky, saved_acts, scales, grad_out, weights, edge_up, edge_down):
    channels, rows, columns = saved_acts.shape
    orders = weights.shape[0]
    blocks = scales.shape[2]
    inner = min(8, sky)
    outer = sky // inner
    norm = 1.0 / math.sqrt(rows * columns * sky)
    stacked = channels * len(TERMS)
    known = channels * TERMS.index((orders - 1, 0))
    edge = 2 * HALO
    vmem = pl.BlockSpec(memory_space=pltpu.VMEM)
    smem = pl.BlockSpec(memory_space=pltpu.SMEM)
    hbm = pl.BlockSpec(memory_space=pltpu.HBM)
    dma = pltpu.SemaphoreType.DMA
    shape = jax.ShapeDtypeStruct
    up, down = jnp.transpose(edge_up, (1, 0, 2)), jnp.transpose(edge_down, (1, 0, 2))
    fields, split, acts, sums, slots, codes, tables, left = pl.pallas_call(
        functools.partial(exchange_kernel, sky),
        out_shape=(
            shape((orders - 1, rows + 2 * HALO, channels, columns), F32),
            shape((rows, stacked, columns), BF16),
            shape((rows, 2 * channels, columns), BF16),
            shape((2 * channels, stacked), F32),
            shape((4, columns // LANES, LANES), jnp.int32),
            shape((4, 3, columns // LANES, LANES), jnp.int32),
            shape((4, 3, 1, columns), jnp.int32),
            shape((channels, stacked), BF16),
        ),
        in_specs=[hbm] * 6,
        out_specs=(vmem,) * 8,
        scratch_shapes=[
            pltpu.VMEM((channels, rows, columns), BF16),
            pltpu.VMEM((channels, rows, blocks), F32),
            pltpu.VMEM((channels, rows, columns), BF16),
            pltpu.VMEM((orders, channels, channels), BF16),
            pltpu.VMEM((channels, rows, columns), F32),
            pltpu.VMEM((rows, channels, columns), F32),
            pltpu.VMEM((rows, channels, blocks), F32),
            pltpu.VMEM((3, columns // LANES, LANES), jnp.int32),
            dma((2, HALO)), dma((2, HALO)), dma((2,)), dma((2,)), dma((channels // 4 + 5,)),
        ],
        compiler_params=pltpu.CompilerParams(
            collective_id=0, has_side_effects=True, vmem_limit_bytes=12 * 2**20
        ),
        name="exchange",
    )(*(pltpu.with_memory_space_constraint(x, pltpu.HBM) for x in (saved_acts, scales, grad_out, weights, up, down)))
    edge_split, second, third, last_links = pl.pallas_call(
        edge_kernel,
        out_shape=(
            shape((edge, stacked, columns), BF16),
            shape((2, HALO, channels, columns), F32),
            shape((2, HALO + 1, channels, columns), F32),
            shape((2, channels, columns), F32),
        ),
        in_specs=[vmem, vmem, smem, vmem, vmem],
        out_specs=(vmem,) * 4,
        scratch_shapes=[
            pltpu.VMEM((orders - 2, 2, HALO + 1, channels, columns), F32),
            pltpu.VMEM((4, channels, columns), F32),
            pltpu.VMEM((4, columns // LANES, channels // 2, LANES), jnp.int32),
        ],
        compiler_params=pltpu.CompilerParams(vmem_limit_bytes=12 * 2**20),
        name="edges",
    )(fields, split, slots, codes, tables)
    rounded, total = pl.pallas_call(
        functools.partial(sum_kernel, sky, inner),
        out_shape=(shape((channels, rows, columns), BF16), shape((channels, stacked), F32)),
        in_specs=[vmem] * 8,
        out_specs=(vmem, vmem),
        scratch_shapes=[
            pltpu.VMEM((channels, rows, columns), F32),
            pltpu.VMEM((2, stacked - known, columns), BF16),
            pltpu.VMEM((inner, channels, stacked), F32),
            pltpu.VMEM((outer, channels, stacked), F32),
            dma((inner,)), dma((inner,)), dma((outer,)), dma((outer,)),
        ],
        compiler_params=pltpu.CompilerParams(
            collective_id=1, has_side_effects=True, vmem_limit_bytes=12 * 2**20
        ),
        name="sky_sum",
    )(split, edge_split, second, third, last_links, acts, sums, left)
    return pl.pallas_call(
        functools.partial(result_kernel, norm),
        out_shape=(shape((channels, rows, columns), BF16), shape((orders, channels, channels), F32)),
        in_specs=[vmem] * 2,
        out_specs=(vmem, vmem),
        compiler_params=pltpu.CompilerParams(vmem_limit_bytes=12 * 2**20),
        name="results",
    )(rounded, total)


def solution(mesh):
    return jax.shard_map(
        functools.partial(on_device, mesh.shape["sky"]),
        mesh=mesh,
        in_specs=(
            P("rep", "sky", None),
            P("rep", "sky", None),
            P("rep", "sky", None),
            P(),
            P("sky", None, None),
            P("sky", None, None),
        ),
        out_specs=(P("rep", "sky", None), P("rep", None, None)),
        check_vma=False,
    )
```
